256 devices in a mesh: seq: 32 (over z_lo, x, core), cam: 4 (over y), tp: 2 (over z_hi).
Axes of the slice: x: 4, y: 4, z: 8 (z_hi: 2, z_lo: 4; z = z_hi * 4 + z_lo), core: 2. Of those that a mesh axis runs over, the one named last changes fastest.
Arguments:
- pixel_feature: bfloat16 [32768, 2048], P(('seq', 'cam'), 'tp'), may hold values from -6 to 6
- depth_score: float32 [32768, 59], P(('seq', 'cam')), may hold values from 0.05 to 5
- depth_bin: int32 [32768, 4], P(('seq', 'cam')), may hold values from 0 to 58
- cell_owner: int32 [131072, 1], P(('seq', 'cam')), may hold values from 0 to 31; in each aligned block of 1024 rows (0 to 1023, 1024 to 2047, ...) at most 64 rows name the same one
- cell_local: int32 [32768, 4], P(('seq', 'cam')), may hold values from 0 to 7
- frame_keep: int32 [64], replicated, may hold values 0 or 1
- norm_gain: float32 [2048], P('tp'), may hold values from 0.1 to 1.9
- w_query: bfloat16 [2048, 2048], P(None, ('cam', 'tp')), may hold values from -1.5 to 1.5
- w_key: bfloat16 [2048, 2048], P(None, ('cam', 'tp')), may hold values from -0.375 to 0.375
- w_value: bfloat16 [2048, 2048], P(None, ('cam', 'tp')), may hold values from -0.125 to 0.125
Outputs:
- attended: bfloat16 [16384, 2048], P('seq', ('cam', 'tp'))
The draws below stay inside these ranges and needn't reach their ends.
Inputs may be any that keep to these rules, and one draw needn't show every extreme that they name: `cell_owner`: among the 1024 points of one index of seq and cam (aligned blocks of rows), no owner is named more than 64 times, a bound that some block reaches.
All inputs are finite; a program needn't handle non-finite values.
Results may differ from the reference program's by a relative error of at most 0.028.
The reference program's roundings to bfloat16 on the way count: a program that leaves them out, or rounds other values in their place, can miss the bound.
Values may be sent and summed in bfloat16 or wider, within the bound.
A program may use at most 64 MiB of HBM per device.

```python
import math
import jax
import jax.numpy as jnp
import numpy as np
from jax import lax

D = 2048
HEADS = 16
HD = 128
DB = 59
KEEP = 4
FR_DEV = 2
CELL_DEV = 8
FRAMES = 64
TOKENS = 16384
PTS_DEV = 1024
PIXELS = 32768
POINTS = 131072
CAP = 64
N_SEQ = 32
N_CAM = 4


def draw_w_query(key, part):
    shape = (D, HEADS * HD)
    values = jnp.clip(jax.random.normal(key, shape, jnp.float32), -6.0, 6.0) * D ** (-0.5)
    return values.astype(jnp.bfloat16)


def with_ends(values, key, low, top_value):
    place = [jax.random.randint(jax.random.fold_in(key, axis), (), 0, length) for axis, length in enumerate(values.shape)]
    widest = values.shape.index(max(values.shape))
    next_to = place[:widest] + [(place[widest] + 1) % values.shape[widest]] + place[widest + 1:]
    return values.at[tuple(place)].set(low).at[tuple(next_to)].set(top_value)


def levels(own_key, extent, pieces, low, top_value):
    level = 1.0
    for axis_at, blocks in pieces:
        draws = jax.random.uniform(jax.random.fold_in(jax.random.fold_in(own_key, 6), axis_at), (blocks,), jnp.float32, low / len(pieces), top_value / len(pieces))
        level = level * jnp.repeat(jnp.exp(draws), extent[axis_at] // blocks).reshape((-1,) + (1,) * (len(extent) - 1 - axis_at))
    return level


def deal_out(stream_key, own, number, rows, count, top, most, skew):
    order = jax.random.permutation(stream_key, count)
    heavy_load, common = shares(count, rows * top, most, skew, True), shares(count, rows * top, most, skew, False)
    places = jnp.arange(count)

    def named(tallies, rotation):
        used = int((tallies > 0).sum())
        fixed = max(1, used // 4)
        moved = fixed + (places - fixed + rotation * (used - fixed)) % max(1, count - fixed)
        return jnp.zeros((count,), jnp.int32).at[order[jnp.where(places < fixed, places, moved)]].set(jnp.asarray(tallies, jnp.int32))

    tallies = jnp.where(number % 4 == 0, named(heavy_load, number // 4), named(common, number - number // 4 - 1))
    mixed = jax.random.permutation(jax.random.fold_in(own, 3), count)
    giver, sink = mixed[0:count // 2 * 2:2], mixed[1:count // 2 * 2:2]
    margin = jnp.minimum(tallies[giver] - 1, most - tallies[sink]) // 2
    margin = jnp.where((giver == order[0]) | (sink == order[0]) | (tallies[sink] == 0), 0, jnp.maximum(margin, 0))
    moved = jax.random.randint(jax.random.fold_in(own, 4), (count // 2,), 0, 1 << 20) % (margin + 1)
    tallies = tallies.at[giver].add(-moved).at[sink].add(moved)
    labels = jnp.searchsorted(jnp.cumsum(tallies), jnp.arange(rows * top), side="right").astype(jnp.int32)
    table = labels.reshape(top, rows).T
    table = table[jax.random.permutation(jax.random.fold_in(own, 1), rows)]
    rotation = jax.random.randint(jax.random.fold_in(own, 2), (rows, 1), 0, top)
    return jnp.take_along_axis(table, (jnp.arange(top)[None, :] + rotation) % top, axis=1)


def shares(count, total, reach, lean, full):
    loads = [(1 << 20) // math.isqrt(standing ** lean) + 1 for standing in range(1, count + 1)]
    largest = reach if full else min(reach, max(-(-total // count), total * loads[0] // sum(loads)))
    least = 1 if total - largest >= count - 1 else 0
    counts, rest = [largest] + [least] * (count - 1), total - largest - least * (count - 1)
    while rest > 0:
        movable = [i for i in range(1, count) if counts[i] < largest] or [i for i in range(1, count) if counts[i] < reach]
        mass, left = sum([loads[i] for i in movable]), rest
        for i in movable:
            more = min(reach - counts[i], max(1, left * loads[i] // mass), rest)
            counts[i] = counts[i] + more
            rest = rest - more
    return np.array(counts)


def bell_draw(key, shape, scale, bound, pieces=(), held_as=jnp.bfloat16):
    entries = scale * jax.random.normal(key, shape, jnp.float32)
    if pieces:
        entries = entries * levels(key, shape, pieces, -0.22, 0.18)
    return jnp.clip(entries, -bound, bound).astype(held_as)


def setup_inputs(seed: int = 0) -> dict:
    keys = jax.random.split(jax.random.key(seed), 11)
    pixel_feature = bell_draw(keys[0], (PIXELS, D), 1.0, 6.0, ((0, 128), (1, 2)))
    depth_score = jnp.clip(jnp.exp(math.log(5.0) - 4.6051702 * jax.random.uniform(keys[1], (PIXELS, DB), jnp.float32) ** levels(keys[1], (PIXELS, DB), ((0, 128),), -0.2, 0.2)), 0.05, 5.0)
    depth_bin = with_ends(jax.random.randint(keys[2], (PIXELS, KEEP), 0, DB), jax.random.fold_in(keys[2], 1), 0, DB - 1).astype(jnp.int32)
    cell_owner_keys = jax.random.split(jax.random.fold_in(keys[3], 1), POINTS // PTS_DEV)
    cell_owner_turns = jax.random.permutation(jax.random.fold_in(keys[3], 3), POINTS // PTS_DEV)
    cell_owner = jax.vmap(lambda own, number: deal_out(jax.random.fold_in(keys[3], 2), own, number, PTS_DEV, N_SEQ, 1, CAP, 2))(cell_owner_keys, cell_owner_turns).reshape((POINTS, 1))
    cell_local = with_ends(jax.random.randint(keys[4], (PIXELS, KEEP), 0, CELL_DEV), jax.random.fold_in(keys[4], 1), 0, CELL_DEV - 1).astype(jnp.int32)
    frame_keep = with_ends((jax.random.randint(keys[5], (FRAMES,), 0, 2) < 1).astype(jnp.int32), jax.random.fold_in(keys[5], 1), 0, 1)
    norm_gain = jnp.clip(1.0 + 0.18 * jax.random.normal(keys[6], (D,), jnp.float32), 0.1, 1.9)
    w_query = draw_w_query(jax.random.fold_in(keys[10], 71), 0)
    w_key = bell_draw(keys[8], (D, HEADS * HD), (D // 9) ** -0.5, 0.375, ((1, 8),))
    w_value = bell_draw(keys[9], (D, HEADS * HD), D ** -0.5, 0.125, ((1, 8),))
    return {"pixel_feature": pixel_feature, "depth_score": depth_score, "depth_bin": depth_bin, "cell_owner": cell_owner, "cell_local": cell_local, "frame_keep": frame_keep, "norm_gain": norm_gain, "w_query": w_query, "w_key": w_key, "w_value": w_value}


def reference(pixel_feature, depth_score, depth_bin, cell_owner, cell_local, frame_keep, norm_gain, w_query, w_key, w_value):
    prob = depth_score / lax.optimization_barrier(jnp.sum(depth_score, axis=1, keepdims=True))
    picked = jnp.take_along_axis(prob, depth_bin, axis=1).astype(jnp.bfloat16)
    weight = lax.optimization_barrier(picked).astype(jnp.float32)
    owner = cell_owner[:, 0].reshape(PIXELS, KEEP)
    point = jnp.arange(POINTS, dtype=jnp.int32).reshape(PIXELS, KEEP)
    frame = point // PTS_DEV // N_CAM * FR_DEV + point % PTS_DEV // (PTS_DEV // FR_DEV)
    token = ((owner * CELL_DEV + cell_local) * FRAMES + frame).astype(jnp.int32)
    feature = pixel_feature.astype(jnp.float32)
    bev = jnp.zeros((TOKENS, D), jnp.float32)
    for k in range(KEEP):
        bev = bev + jax.ops.segment_sum(feature * weight[:, k:k + 1], token[:, k], num_segments=TOKENS)
    square_mean = lax.optimization_barrier(jnp.mean(bev * bev, axis=1, keepdims=True))
    normed = (bev * lax.rsqrt(square_mean + 1e-05) * norm_gain).astype(jnp.bfloat16)
    query = jnp.dot(normed, w_query, preferred_element_type=jnp.float32).astype(jnp.bfloat16)
    key = jnp.dot(normed, w_key, preferred_element_type=jnp.float32).astype(jnp.bfloat16)
    value = jnp.dot(normed, w_value, preferred_element_type=jnp.float32).astype(jnp.bfloat16)
    query = query.reshape(TOKENS, HEADS, HD).transpose(1, 0, 2)
    key = key.reshape(TOKENS, HEADS, HD).transpose(1, 0, 2)
    value = value.reshape(TOKENS, HEADS, HD).transpose(1, 0, 2)
    frames_of = jnp.arange(TOKENS, dtype=jnp.int32) % FRAMES
    kept = frame_keep[frames_of]
    scale = 1.0 / HD ** 0.5

    def one_head(operands):
        head_query, head_key, head_value = operands
        allowed = (frames_of[None, :] <= frames_of[:, None]) & ((kept[None, :] > 0) | (frames_of[None, :] == frames_of[:, None]))
        scores = jnp.dot(head_query, head_key.T, preferred_element_type=jnp.float32) * scale
        peak = lax.optimization_barrier(jnp.max(jnp.where(allowed, scores, -1e+30), axis=1, keepdims=True))
        expo = jnp.where(allowed, jnp.exp(scores - peak), 0.0)
        total = lax.optimization_barrier(jnp.sum(expo, axis=1, keepdims=True))
        mixed = jnp.dot(expo.astype(jnp.bfloat16), head_value, preferred_element_type=jnp.float32)
        return mixed / total
    heads_out = lax.map(one_head, (query, key, value))
    return heads_out.transpose(1, 0, 2).reshape(TOKENS, HEADS * HD).astype(jnp.bfloat16)
```

```python
import functools
import math

import jax
import jax.numpy as jnp
from jax import lax
from jax.experimental import pallas as pl
from jax.experimental.pallas import tpu as pltpu
from jax.sharding import PartitionSpec as P

MESH = pl.DeviceIdType.MESH
D = 2048
HALF = 1024
HD = 128
EPS = 1e-05
PIX = 256
CELLS = 256
TOK = 512
CH = 4
ROWS = PIX // CH
BF = jnp.bfloat16
F32 = jnp.float32


def where_am_i():
    seq = lax.axis_index("seq")
    cam = lax.axis_index("cam")
    tp = lax.axis_index("tp")
    z_lo = seq // 8
    x = lax.rem(seq // 2, 4)
    core = lax.rem(seq, 2)
    return seq, cam, tp, z_lo, x, core


def gather_project(
    x_ref, meta_ref, gain_ref, wq_hbm, wk_hbm, wv_hbm, q_ref, kv_ref,
    xg, metag, gaing, ru, rd, w_s, bev, nrm,
    xsend, xrecv, zsend, zrecv, psend, precv, fsend, msend, mrecv, gsend, grecv, lsem,
):
    seq, cam, tp, z_lo, x, core = where_am_i()
    z = tp * 4 + z_lo
    up, down = lax.rem(cam + 1, 4), lax.rem(cam + 3, 4)
    across = lax.rem(cam + 2, 4)

    def at_y(c):
        return (seq, c, tp)

    def at_z(step):
        zz = lax.rem(z + step + 8, 8)
        return (lax.rem(zz, 4) * 8 + lax.rem(seq, 8), cam, zz // 4)

    barrier = pltpu.get_barrier_semaphore()
    peers = [at_y(up), at_y(down), at_y(across), at_z(1), at_z(-1), at_z(3), at_z(-3), at_z(4)]
    for peer in peers:
        pl.semaphore_signal(barrier, inc=1, device_id=peer, device_id_type=MESH)

    loads = []
    for n, w in enumerate((wq_hbm, wk_hbm, wv_hbm)):
        loads.append(pltpu.make_async_copy(w, w_s.at[n], lsem.at[n]))
    loads.append(pltpu.make_async_copy(meta_ref, metag.at[0], lsem.at[3]))
    loads.append(pltpu.make_async_copy(gain_ref, gaing.at[0], lsem.at[4]))
    for half in range(2):
        loads.append(
            pltpu.make_async_copy(x_ref.at[half], xg.at[0, half, 0], lsem.at[5 + half])
        )
    for load in loads:
        load.start()
    pl.semaphore_wait(barrier, len(peers))

    def remote(src, dst, send, recv, device):
        copy = pltpu.make_async_remote_copy(
            src_ref=src, dst_ref=dst, send_sem=send, recv_sem=recv, device_id=device,
            device_id_type=MESH,
        )
        copy.start()
        return copy

    def piece(ref, c):
        return ref.at[pl.ds((c % 2) * ROWS, ROWS)]

    sent = []
    for c in (0, 2, 1, 3):
        target = ru if c < 2 else rd
        sent.append(
            remote(
                piece(x_ref.at[c // 2], c), target.at[c % 2], zsend.at[c], zrecv.at[c],
                at_z(1) if c < 2 else at_z(-1),
            )
        )

    def spread(source, p, c, toward):
        rel = 3 if toward == 0 else 1
        sent.append(
            remote(
                source, piece(xg.at[p, c // 2, rel], c), xsend.at[p, toward, c],
                xrecv.at[p, rel, c], at_y(up if toward == 0 else down),
            )
        )

    def arrived(p, rel, c):
        ref = piece(xg.at[p, c // 2, rel], c)
        pltpu.make_async_remote_copy(
            src_ref=ref, dst_ref=ref, send_sem=xsend.at[p, 0, c], recv_sem=xrecv.at[p, rel, c],
            device_id=at_y(up), device_id_type=MESH,
        ).wait_recv()

    def forward(p, rel, c):
        ref = piece(xg.at[p, c // 2, rel], c)
        sent.append(
            remote(
                ref, piece(xg.at[p, c // 2, 2], c), fsend.at[p, c], xrecv.at[p, 2, c],
                at_y(down if rel == 1 else up),
            )
        )

    sent.append(remote(meta_ref, metag.at[3], msend.at[0], mrecv.at[0], at_y(up)))
    sent.append(remote(meta_ref, metag.at[1], msend.at[1], mrecv.at[1], at_y(down)))
    sent.append(remote(meta_ref, metag.at[2], msend.at[2], mrecv.at[2], at_y(across)))
    sent.append(remote(gain_ref, gaing.at[1], gsend, grecv, at_z(4)))
    for n in range(4):
        spread(piece(x_ref.at[(2, 3, 0, 1)[n] // 2], n), 0, (2, 3, 0, 1)[n], 0)
        spread(piece(x_ref.at[n // 2], n), 0, n, 1)

    def relay(c):
        target = ru if c < 2 else rd
        ref = target.at[c % 2]
        pltpu.make_async_remote_copy(
            src_ref=ref, dst_ref=ref, send_sem=zsend.at[c], recv_sem=zrecv.at[c],
            device_id=at_z(1), device_id_type=MESH,
        ).wait_recv()
        sent.append(
            remote(
                ref, piece(xg.at[1, c // 2, 0], c), psend.at[c], precv.at[c],
                at_z(3) if c < 2 else at_z(-3),
            )
        )

    def partner(c):
        ref = piece(xg.at[1, c // 2, 0], c)
        pltpu.make_async_remote_copy(
            src_ref=ref, dst_ref=ref, send_sem=psend.at[c], recv_sem=precv.at[c],
            device_id=at_z(3), device_id_type=MESH,
        ).wait_recv()
        spread(ref, 1, c, 0)
        spread(ref, 1, c, 1)

    for c in (0, 2, 1, 3):
        relay(c)
    for c in (2, 3):
        arrived(0, 3, c)
        forward(0, 3, c)
        arrived(0, 1, c - 2)
        forward(0, 1, c - 2)
    for c in (0, 2, 1, 3):
        partner(c)

    for n, (rel, _) in enumerate(((3, 0), (1, 1), (2, 2))):
        pltpu.make_async_remote_copy(
            src_ref=meta_ref, dst_ref=metag.at[rel], send_sem=msend.at[n], recv_sem=mrecv.at[n],
            device_id=at_y(up), device_id_type=MESH,
        ).wait_recv()
    for load in loads:
        load.wait()

    token = lax.broadcasted_iota(jnp.int32, (CELLS, 128), 0).astype(F32)

    def mixing(half):
        high, low = [], []
        for rel in range(4):
            block = metag[rel][:, half * 128 : half * 128 + 128]
            total = jnp.zeros((CELLS, 128), F32)
            for k in range(4):
                hit = token == block[4 + k : 5 + k, :]
                total = total + jnp.where(hit, block[k : k + 1, :], 0.0)
            first = total.astype(BF)
            high.append(first)
            low.append((total - first.astype(F32)).astype(BF))
        return jnp.concatenate(high, axis=1), jnp.concatenate(low, axis=1)

    mixes = [mixing(0), mixing(1)]

    def pool(p, half):
        rows = xg[p, half].reshape(4 * 128, HALF)
        high, low = mixes[half]
        bev[p, half * CELLS : half * CELLS + CELLS, :] = jnp.dot(
            high, rows, preferred_element_type=F32
        ) + jnp.dot(low, rows, preferred_element_type=F32)

    for c in range(4):
        arrived(0, 3 if c < 2 else 1, c)
    for c in range(4):
        arrived(0, 2, c)
    pool(0, 0)
    pool(0, 1)
    for c in (2, 3):
        arrived(1, 3, c)
        forward(1, 3, c)
        arrived(1, 1, c - 2)
        forward(1, 1, c - 2)
    for c in range(4):
        arrived(1, 3 if c < 2 else 1, c)
    for c in range(4):
        arrived(1, 2, c)
    pool(1, 0)
    pool(1, 1)
    pltpu.make_async_remote_copy(
        src_ref=gain_ref, dst_ref=gaing.at[1], send_sem=gsend, recv_sem=grecv,
        device_id=at_z(4), device_id_type=MESH,
    ).wait_recv()
    step = 128
    for n in range(TOK // step):
        a = bev[0, n * step : (n + 1) * step, :]
        b = bev[1, n * step : (n + 1) * step, :]
        squares = jnp.sum(a * a + b * b, axis=1, keepdims=True)
        scale = lax.rsqrt(squares / D + EPS)
        nrm[0, n * step : (n + 1) * step, :] = (a * scale * gaing[0]).astype(BF)
        nrm[1, n * step : (n + 1) * step, :] = (b * scale * gaing[1]).astype(BF)
    own = pl.multiple_of(tp * HALF, HALF)
    other = pl.multiple_of((1 - tp) * HALF, HALF)
    for n in range(3):
        result = jnp.dot(nrm[0], w_s[n, pl.ds(own, HALF), :], preferred_element_type=F32)
        result = result + jnp.dot(
            nrm[1], w_s[n, pl.ds(other, HALF), :], preferred_element_type=F32
        )
        result = result.astype(BF)
        for h in range(2):
            part = result[:, h * HD : (h + 1) * HD]
            if n == 0:
                q_ref[h] = part
            else:
                kv_ref[h, n - 1] = part
    for copy in sent:
        copy.wait_send()


def plane_gather(
    q_ref, kv_ref, qg, kvg,
    presend, prerecv, qsend, qrecv, zsend, zrecv, xsend, xrecv, fsend, csend, crecv, lsem,
):
    seq, cam, tp, z, x, core = where_am_i()
    head = lax.rem(z, 2)

    def flip(value, bit):
        low, high = lax.rem(value, 2), value // 2
        low = 1 - low if bit & 1 else low
        high = 1 - high if bit & 2 else high
        return high * 2 + low

    def device(zz, xx, cc):
        return (zz * 8 + xx * 2 + cc, cam, tp)

    def index(zz, xx, cc):
        return zz * 8 + xx * 2 + cc

    right, left, far = lax.rem(x + 1, 4), lax.rem(x + 3, 4), lax.rem(x + 2, 4)
    z1, z2 = flip(z, 1), flip(z, 2)
    sib = 1 - core
    peers = [
        device(z1, x, core), device(z2, x, core), device(z, right, core), device(z, left, core),
        device(z, x, sib),
    ]
    barrier = pltpu.get_barrier_semaphore()
    for peer in peers:
        pl.semaphore_signal(barrier, inc=1, device_id=peer, device_id_type=MESH)
    me = index(z, x, core)
    local = [
        pltpu.make_async_copy(q_ref.at[head], qg.at[head], lsem.at[0]),
        pltpu.make_async_copy(kv_ref.at[head], kvg.at[me], lsem.at[1]),
    ]
    for copy in local:
        copy.start()
    pl.semaphore_wait(barrier, len(peers))
    sent = []

    def remote(src, dst, send, recv, dev):
        copy = pltpu.make_async_remote_copy(
            src_ref=src, dst_ref=dst, send_sem=send, recv_sem=recv, device_id=dev,
            device_id_type=MESH,
        )
        copy.start()
        sent.append(copy)

    def received(ref, send, recv):
        pltpu.make_async_remote_copy(
            src_ref=ref, dst_ref=ref, send_sem=send, recv_sem=recv,
            device_id=device(z, x, sib), device_id_type=MESH,
        ).wait_recv()

    def unit(dz, dx, cc=None):
        zz = z if dz == 0 else flip(z, dz)
        xx = (x, right, far, left)[dx]
        return index(zz, xx, core if cc is None else cc)

    remote(kv_ref.at[1 - head], kvg.at[me], presend, prerecv, device(z1, x, core))
    remote(kv_ref.at[head], kvg.at[me], zsend.at[0], zrecv.at[0], device(z2, x, core))

    def spread(dz):
        u = unit(dz, 0)
        src = kv_ref.at[head] if dz == 0 else kvg.at[u]
        for order in range(2):
            for toward in range(2):
                half = 1 - order if toward == 0 else order
                rel = 3 if toward == 0 else 1
                remote(
                    src.at[half], kvg.at[u, half], xsend.at[dz, toward, half],
                    xrecv.at[dz, rel, half], device(z, right if toward == 0 else left, core),
                )
        for half in range(2):
            remote(
                src.at[half], kvg.at[u, half], csend.at[dz, 0, half], crecv.at[dz, 0, half],
                device(z, x, sib),
            )

    def arrived(dz, rel, half):
        received(kvg.at[unit(dz, rel), half], xsend.at[dz, 0, half], xrecv.at[dz, rel, half])

    def share(dz, rel, half):
        u = unit(dz, rel)
        remote(
            kvg.at[u, half], kvg.at[u, half], csend.at[dz, rel, half], crecv.at[dz, rel, half],
            device(z, x, sib),
        )

    def forward(dz):
        for rel, half in ((3, 1), (1, 0)):
            arrived(dz, rel, half)
            u = unit(dz, rel)
            remote(
                kvg.at[u, half], kvg.at[u, half], fsend.at[dz, half], xrecv.at[dz, 2, half],
                device(z, right if rel == 3 else left, core),
            )
            share(dz, rel, half)

    spread(0)
    remote(q_ref.at[1 - head], qg.at[head], qsend, qrecv, device(z1, x, core))
    received(kvg.at[unit(1, 0)], presend, prerecv)
    remote(
        kvg.at[unit(1, 0)], kvg.at[unit(1, 0)], zsend.at[1], zrecv.at[1], device(z2, x, core)
    )
    spread(1)
    forward(0)
    received(kvg.at[unit(2, 0)], zsend.at[0], zrecv.at[0])
    spread(2)
    forward(1)
    received(kvg.at[unit(3, 0)], zsend.at[1], zrecv.at[1])
    spread(3)
    forward(2)
    for dz in range(3):
        for rel, half in ((3, 0), (1, 1), (2, 0), (2, 1)):
            arrived(dz, rel, half)
            share(dz, rel, half)
    forward(3)
    for rel, half in ((3, 0), (1, 1), (2, 0), (2, 1)):
        arrived(3, rel, half)
        share(3, rel, half)
    received(qg.at[1 - head], qsend, qrecv)
    for dz in range(4):
        for rel in range(4):
            for half in range(2):
                received(
                    kvg.at[unit(dz, rel, sib), half], csend.at[dz, rel, half],
                    crecv.at[dz, rel, half],
                )
    for copy in local:
        copy.wait()
    for copy in sent:
        copy.wait_send()


SCALE = math.log2(math.e) / math.sqrt(HD)


def attention(frame_ref, kept_ref, count_ref, keep_ref, q_ref, kv_ref, o_ref, acc, top, tot):
    def block(q, rows, g, mask_from):
        unit, off = g // 2, pl.multiple_of(lax.rem(g, 2) * CELLS, CELLS)
        keys = kv_ref[unit, 0, pl.ds(off, CELLS), :]
        values = kv_ref[unit, 1, pl.ds(off, CELLS), :]
        s = lax.dot_general(q, keys, (((1,), (1,)), ((), ())), preferred_element_type=F32)
        before = top[rows, :]
        peak = jnp.maximum(before, jnp.max(s, axis=1, keepdims=True))
        factor = jnp.exp2((before - peak) * SCALE)
        e = jnp.exp2((s - jnp.concatenate([peak, peak], axis=1)) * SCALE)
        mixed = jnp.dot(e.astype(BF), values, preferred_element_type=F32)
        top[rows, :] = peak
        tot[rows, :] = tot[rows, :] * factor + (e[:, :128] + e[:, 128:])
        acc[rows, :] = acc[rows, :] * factor + mixed

    for b in range(2):
        frame = frame_ref[b]
        top[...] = jnp.full(top.shape, -1e30, F32)
        tot[...] = jnp.zeros(tot.shape, F32)
        acc[...] = jnp.zeros(acc.shape, F32)
        lower, upper = pl.ds(0, CELLS), pl.ds(CELLS, CELLS)
        block(q_ref[b, 0:CELLS, :], lower, frame, None)
        block(q_ref[b, CELLS:TOK, :], upper, frame + 1, None)

        @pl.when(keep_ref[frame] > 0)
        def _():
            block(q_ref[b, CELLS:TOK, :], upper, frame, None)

        @pl.loop(0, count_ref[frame])
        def _(i):
            block(q_ref[b], pl.ds(0, TOK), kept_ref[i], None)

        outs = []
        for f in range(2):
            rows = slice(f * CELLS, (f + 1) * CELLS)
            total = jnp.sum(tot[rows, :], axis=1, keepdims=True)
            outs.append((acc[rows, :] / total).reshape(32, 8, HD))
        o_ref[:, b] = jnp.concatenate(outs, axis=1).astype(BF)


def to_owner(o_ref, r_ref, send, recv, lsem):
    seq, cam, tp, z, x, core = where_am_i()
    barrier = pltpu.get_barrier_semaphore()

    @pl.loop(1, 32)
    def _(d):
        peer = lax.rem(seq + d, 32)
        pl.semaphore_signal(barrier, inc=1, device_id=(peer, cam, tp), device_id_type=MESH)

    local = pltpu.make_async_copy(o_ref.at[seq], r_ref.at[seq], lsem)
    local.start()
    pl.semaphore_wait(barrier, 31)

    def push(d):
        peer = lax.rem(seq + d, 32)
        return pltpu.make_async_remote_copy(
            src_ref=o_ref.at[peer], dst_ref=r_ref.at[seq], send_sem=send.at[d],
            recv_sem=recv.at[d], device_id=(peer, cam, tp), device_id_type=MESH,
        )

    @pl.loop(1, 32)
    def _(d):
        push(d).start()

    @pl.loop(1, 32)
    def _(d):
        source = lax.rem(seq + 32 - d, 32)
        pltpu.make_async_remote_copy(
            src_ref=o_ref.at[source], dst_ref=r_ref.at[source], send_sem=send.at[d],
            recv_sem=recv.at[d], device_id=(source, cam, tp), device_id_type=MESH,
        ).wait_recv()

    @pl.loop(1, 32)
    def _(d):
        push(d).wait_send()

    local.wait()


VMEM = pl.BlockSpec(memory_space=pltpu.VMEM)
ANY = pl.BlockSpec(memory_space=pl.ANY)
SMEM = pl.BlockSpec(memory_space=pltpu.SMEM)
DMA = pltpu.SemaphoreType.DMA
LIMIT = 60 * 1024 * 1024


def call_gather(x, meta, gain, wq, wk, wv):
    return pl.pallas_call(
        gather_project,
        out_shape=(
            jax.ShapeDtypeStruct((2, TOK, HD), BF),
            jax.ShapeDtypeStruct((2, 2, TOK, HD), BF),
        ),
        in_specs=[VMEM, VMEM, VMEM, ANY, ANY, ANY],
        out_specs=(VMEM, VMEM),
        scratch_shapes=[
            pltpu.VMEM((2, 2, 4, 128, HALF), BF),
            pltpu.VMEM((4, 8, PIX), F32),
            pltpu.VMEM((2, 1, HALF), F32),
            pltpu.VMEM((2, ROWS, HALF), BF),
            pltpu.VMEM((2, ROWS, HALF), BF),
            pltpu.VMEM((3, D, 2 * HD), BF),
            pltpu.VMEM((2, TOK, HALF), F32),
            pltpu.VMEM((2, TOK, HALF), BF),
            DMA((2, 2, 4)), DMA((2, 4, 4)), DMA((4,)), DMA((4,)), DMA((4,)), DMA((4,)),
            DMA((2, 4)), DMA((3,)), DMA((3,)), DMA, DMA, DMA((7,)),
        ],
        compiler_params=pltpu.CompilerParams(
            collective_id=0, has_side_effects=True, vmem_limit_bytes=LIMIT
        ),
        name="gather_project",
    )(x, meta, gain, wq, wk, wv)


def call_plane(q, kv):
    return pl.pallas_call(
        plane_gather,
        out_shape=(
            jax.ShapeDtypeStruct((2, TOK, HD), BF),
            jax.ShapeDtypeStruct((32, 2, TOK, HD), BF),
        ),
        in_specs=[VMEM, VMEM],
        out_specs=(ANY, ANY),
        scratch_shapes=[
            DMA, DMA, DMA, DMA, DMA((2,)), DMA((2,)), DMA((4, 2, 2)), DMA((4, 4, 2)),
            DMA((4, 2)), DMA((4, 4, 2)), DMA((4, 4, 2)), DMA((2,)),
        ],
        compiler_params=pltpu.CompilerParams(
            collective_id=1, has_side_effects=True, vmem_limit_bytes=LIMIT
        ),
        name="plane_gather",
    )(q, kv)


def call_attention(frames, kept, counts, keep, qg, kvg):
    return pl.pallas_call(
        attention,
        out_shape=jax.ShapeDtypeStruct((32, 2, 16, HD), BF),
        in_specs=[SMEM, SMEM, SMEM, SMEM, VMEM, VMEM],
        out_specs=VMEM,
        scratch_shapes=[
            pltpu.VMEM((TOK, HD), F32), pltpu.VMEM((TOK, HD), F32), pltpu.VMEM((TOK, HD), F32),
        ],
        compiler_params=pltpu.CompilerParams(vmem_limit_bytes=LIMIT),
        name="attention",
    )(frames, kept, counts, keep, qg, kvg)


def call_owner(o):
    return pl.pallas_call(
        to_owner,
        out_shape=jax.ShapeDtypeStruct((32, 2, 16, HD), BF),
        in_specs=[VMEM],
        out_specs=VMEM,
        scratch_shapes=[DMA((32,)), DMA((32,)), DMA],
        compiler_params=pltpu.CompilerParams(
            collective_id=2, has_side_effects=True, vmem_limit_bytes=LIMIT
        ),
        name="to_owner",
    )(o)


def local(
    pixel_feature, depth_score, depth_bin, cell_owner, cell_local, frame_keep, norm_gain,
    w_query, w_key, w_value,
):
    seq = lax.axis_index("seq")
    prob = depth_score / jnp.sum(depth_score, axis=1, keepdims=True)
    bins = jnp.arange(depth_score.shape[1], dtype=jnp.int32)
    picked = jnp.sum(
        jnp.where(depth_bin[:, :, None] == bins[None, None, :], prob[:, None, :], 0.0), axis=2
    )
    weight = lax.reduce_precision(picked, 8, 7)
    cell = (cell_owner.reshape(PIX, 4) * 8 + cell_local).astype(F32)
    meta = jnp.concatenate([weight, cell], axis=1).T
    q, kv = call_gather(
        pixel_feature.reshape(2, 128, HALF), meta, norm_gain.reshape(1, HALF), w_query, w_key,
        w_value,
    )
    qg, kvg = call_plane(q, kv)
    keep = (frame_keep > 0).astype(jnp.int32)
    order = jnp.cumsum(keep) - keep
    frames = jnp.arange(64, dtype=jnp.int32)
    kept = jnp.sum(
        jnp.where((order[None, :] == frames[:, None]) & (keep[None, :] > 0), frames[None, :], 0),
        axis=1,
    )
    pair = (seq // 16) * 16 + lax.rem(seq, 8) + jnp.array([0, 8], jnp.int32)
    o = call_attention(pair * 2, kept, order, keep, qg, kvg)
    r = call_owner(o)
    r = r.reshape(2, 2, 8, 2, 2, 8, HD)
    out = r.transpose(5, 0, 3, 2, 4, 1, 6)
    return out.reshape(TOK, 2 * HD)


def solution(mesh):
    return jax.shard_map(
        local,
        mesh=mesh,
        in_specs=(
            P(("seq", "cam"), "tp"),
            P(("seq", "cam"), None),
            P(("seq", "cam"), None),
            P(("seq", "cam"), None),
            P(("seq", "cam"), None),
            P(),
            P("tp"),
            P(None, ("cam", "tp")),
            P(None, ("cam", "tp")),
            P(None, ("cam", "tp")),
        ),
        out_specs=P("seq", ("cam", "tp")),
        check_vma=False,
    )
```

```python
import functools
import math

import jax
import jax.numpy as jnp
from jax import lax
from jax.experimental import pallas as pl
from jax.experimental.pallas import tpu as pltpu
from jax.sharding import PartitionSpec as P

MESH = pl.DeviceIdType.MESH
D = 2048
HALF = 1024
HD = 128
EPS = 1e-05
PIX = 256
CELLS = 256
TOK = 512
CH = 4
ROWS = PIX // CH
BF = jnp.bfloat16
F32 = jnp.float32


def where_am_i():
    seq = lax.axis_index("seq")
    cam = lax.axis_index("cam")
    tp = lax.axis_index("tp")
    z_lo = seq // 8
    x = lax.rem(seq // 2, 4)
    core = lax.rem(seq, 2)
    return seq, cam, tp, z_lo, x, core


SCALE = math.log2(math.e) / math.sqrt(HD)
FAR = -1e30
START = -0.5e30


def fused(
    x_ref, meta_ref, gain_ref, keep_ref, wq_hbm, wk_hbm, wv_hbm, r_ref,
    xg, metag, gaing, ru, rd, w_s, bev, nrm, mix, kvb, kvs, qb, acc, top, tot, ob,
    xsend, xrecv, zsend, zrecv, psend, precv, fsend, msend, mrecv, gsend, grecv, lsem,
    bpre_s, bpre_r, bq_s, bq_r, bz_s, bz_r, bx_s, bx_r, bf_s, bc_s, bc_r, lc, d_s, d_r, ld,
):
    seq, cam, tp, z_lo, x, core = where_am_i()
    z = tp * 4 + z_lo
    up, down = lax.rem(cam + 1, 4), lax.rem(cam + 3, 4)
    across = lax.rem(cam + 2, 4)
    head = z_lo // 2

    def at_y(c):
        return (seq, c, tp)

    def at_z(step):
        zz = lax.rem(z + step + 8, 8)
        return (lax.rem(zz, 4) * 8 + lax.rem(seq, 8), cam, zz // 4)

    def flip(zz, dz):
        low = lax.rem(lax.rem(zz, 2) + (dz + 1) // 2, 2)
        high = lax.rem(zz // 2 + dz, 2)
        return high * 2 + low

    def index(zz, xx, cc):
        return zz * 8 + xx * 2 + cc

    def plane(zz, xx, cc):
        return (index(zz, xx, cc), cam, tp)

    right, left = lax.rem(x + 1, 4), lax.rem(x + 3, 4)
    sib = 1 - core
    z3, z1 = flip(z_lo, 1), flip(z_lo, 2)

    barrier = pltpu.get_barrier_semaphore()
    peers = [at_y(up), at_y(down), at_y(across), at_z(1), at_z(-1), at_z(3), at_z(-3), at_z(4)]
    for peer in peers:
        pl.semaphore_signal(barrier, inc=1, device_id=peer, device_id_type=MESH)

    @pl.loop(1, 32)
    def _(d):
        pl.semaphore_signal(
            barrier, inc=1, device_id=(lax.rem(seq + d, 32), cam, tp), device_id_type=MESH
        )

    loads = []
    for n, w in enumerate((wq_hbm, wk_hbm, wv_hbm)):
        loads.append(pltpu.make_async_copy(w, w_s.at[n], lsem.at[n]))
    loads.append(pltpu.make_async_copy(meta_ref, metag.at[0], lsem.at[3]))
    loads.append(pltpu.make_async_copy(gain_ref, gaing.at[0], lsem.at[4]))
    for half in range(2):
        loads.append(
            pltpu.make_async_copy(x_ref.at[half], xg.at[0, half, 0], lsem.at[5 + half])
        )
    for load in loads:
        load.start()
    acc[...] = jnp.zeros(acc.shape, F32)
    tot[...] = jnp.zeros(tot.shape, F32)
    top[...] = jnp.full(top.shape, START, F32)
    pl.semaphore_wait(barrier, len(peers) + 31)

    sent = []

    def describe(src, dst, send, recv, device):
        return pltpu.make_async_remote_copy(
            src_ref=src, dst_ref=dst, send_sem=send, recv_sem=recv, device_id=device,
            device_id_type=MESH,
        )

    def remote(src, dst, send, recv, device):
        copy = describe(src, dst, send, recv, device)
        copy.start()
        sent.append(copy)

    def received(ref, send, recv):
        describe(ref, ref, send, recv, at_y(up)).wait_recv()

    def piece(ref, c):
        return ref.at[pl.ds((c % 2) * ROWS, ROWS)]

    def z_out(f):
        for e in range(2):
            c = 2 * f + e
            target = ru if e == 0 else rd
            remote(
                piece(x_ref.at[f], c), target.at[f], zsend.at[c], zrecv.at[c],
                at_z(1) if e == 0 else at_z(-1),
            )

    def relay(f):
        for e in range(2):
            c = 2 * f + e
            ref = (ru if e == 0 else rd).at[f]
            received(ref, zsend.at[c], zrecv.at[c])
            remote(
                ref, piece(xg.at[1, f, 0], c), psend.at[c], precv.at[c],
                at_z(3) if e == 0 else at_z(-3),
            )

    def spread_y(source, p, c, toward):
        rel = 3 if toward == 0 else 1
        remote(
            source, piece(xg.at[p, c // 2, rel], c), xsend.at[p, toward, c],
            xrecv.at[p, rel, c], at_y(up if toward == 0 else down),
        )

    def own_y(f):
        for e in range(2):
            for toward in range(2):
                c = 2 * f + (1 - e if toward == 0 else e)
                spread_y(piece(x_ref.at[f], c), 0, c, toward)

    def got(p, rel, c):
        received(piece(xg.at[p, c // 2, rel], c), xsend.at[p, 0, c], xrecv.at[p, rel, c])

    def forward_y(p, f):
        for rel, c in ((3, 2 * f + 1), (1, 2 * f)):
            got(p, rel, c)
            ref = piece(xg.at[p, f, rel], c)
            remote(
                ref, piece(xg.at[p, f, 2], c), fsend.at[p, c], xrecv.at[p, 2, c],
                at_y(down if rel == 1 else up),
            )

    def rest_y(p, f):
        got(p, 3, 2 * f)
        got(p, 1, 2 * f + 1)
        got(p, 2, 2 * f)
        got(p, 2, 2 * f + 1)

    def partner(f):
        for e in range(2):
            c = 2 * f + e
            received(piece(xg.at[1, f, 0], c), psend.at[c], precv.at[c])
        for e in range(2):
            for toward in range(2):
                c = 2 * f + (1 - e if toward == 0 else e)
                spread_y(piece(xg.at[1, f, 0], c), 1, c, toward)

    def build_mixing(half):
        token = lax.broadcasted_iota(jnp.int32, (CELLS, 128), 0).astype(F32)
        for rel in range(4):
            block = metag[rel][:, half * 128 : half * 128 + 128]
            total = jnp.zeros((CELLS, 128), F32)
            for k in range(4):
                hit = token == block[4 + k : 5 + k, :]
                total = total + jnp.where(hit, block[k : k + 1, :], 0.0)
            first = total.astype(BF)
            mix[half, 0, :, rel * 128 : rel * 128 + 128] = first
            mix[half, 1, :, rel * 128 : rel * 128 + 128] = (
                total - first.astype(F32)
            ).astype(BF)

    def pool(p, f):
        rows = xg[p, f].reshape(4 * 128, HALF)
        bev[p, f] = jnp.dot(mix[f, 0], rows, preferred_element_type=F32) + jnp.dot(
            mix[f, 1], rows, preferred_element_type=F32
        )

    own = pl.multiple_of(tp * HALF, HALF)
    other = pl.multiple_of((1 - tp) * HALF, HALF)
    me = seq

    def project(f):
        step = 128
        for n in range(CELLS // step):
            a = bev[0, f, n * step : (n + 1) * step, :]
            b = bev[1, f, n * step : (n + 1) * step, :]
            squares = jnp.sum(a * a + b * b, axis=1, keepdims=True)
            scale = lax.rsqrt(squares / D + EPS)
            nrm[0, n * step : (n + 1) * step, :] = (a * scale * gaing[0]).astype(BF)
            nrm[1, n * step : (n + 1) * step, :] = (b * scale * gaing[1]).astype(BF)
        for n in (1, 2, 0):
            result = jnp.dot(nrm[0], w_s[n, pl.ds(own, HALF), :], preferred_element_type=F32)
            result = result + jnp.dot(
                nrm[1], w_s[n, pl.ds(other, HALF), :], preferred_element_type=F32
            )
            result = result.astype(BF)
            for h in range(2):
                part = result[:, h * HD : (h + 1) * HD]
                mine = lax.rem(head + h, 2)
                if n == 0:
                    qb[mine * 2, f] = part
                else:
                    kvs[mine, f, n - 1] = part

    def own_copies(f):
        return [
            describe(kvs.at[1, f], kvb.at[me, f], bpre_s.at[f], bpre_r.at[f], plane(z3, x, core)),
            describe(
                kvs.at[0, f], kvb.at[me, f], bz_s.at[f, 0], bz_r.at[f, 0], plane(z1, x, core)
            ),
            describe(qb.at[2, f], qb.at[1, f], bq_s.at[f], bq_r.at[f], plane(z3, x, core)),
        ]

    def issue_own(f):
        keep_copy = pltpu.make_async_copy(kvs.at[0, f], kvb.at[me, f], lc.at[f])
        keep_copy.start()
        for copy in own_copies(f):
            copy.start()
        keep_copy.wait()

    def unit(dz, dx, cc):
        return index(flip(z_lo, dz), lax.rem(x + dx, 4), cc)

    def x_copy(n, toward, kv):
        ref = kvb.at[unit(lax.rem(n, 4), 0, core), n // 4, kv]
        return describe(
            ref, ref, bx_s.at[n, toward, kv], bx_r.at[n, 3 if toward == 0 else 1, kv],
            plane(z_lo, right if toward == 0 else left, core),
        )

    def f_copy(n, kv):
        ref = kvb.at[unit(lax.rem(n, 4), 3 if kv == 1 else 1, core), n // 4, kv]
        return describe(
            ref, ref, bf_s.at[n, kv], bx_r.at[n, 2, kv],
            plane(z_lo, right if kv == 1 else left, core),
        )

    def c_copy(n, dx):
        ref = kvb.at[unit(lax.rem(n, 4), dx, core), n // 4]
        return describe(ref, ref, bc_s.at[n, dx], bc_r.at[n, dx], plane(z_lo, x, sib))

    def z_copy(f):
        ref = kvb.at[unit(1, 0, core), f]
        return describe(ref, ref, bz_s.at[f, 1], bz_r.at[f, 1], plane(z1, x, core))

    def arrived(n, rel, kv):
        ref = kvb.at[unit(lax.rem(n, 4), rel, core), n // 4, kv]
        received(ref, bx_s.at[n, 0, kv], bx_r.at[n, rel, kv])

    def stage0(n):
        f, dz = n // 4, lax.rem(n, 4)

        @pl.when(dz == 1)
        def _():
            received(kvb.at[unit(1, 0, core), f], bpre_s.at[f], bpre_r.at[f])
            z_copy(f).start()
            received(qb.at[1, f], bq_s.at[f], bq_r.at[f])

        @pl.when(dz == 2)
        def _():
            received(kvb.at[unit(2, 0, core), f], bz_s.at[f, 0], bz_r.at[f, 0])

        @pl.when(dz == 3)
        def _():
            received(kvb.at[unit(3, 0, core), f], bz_s.at[f, 1], bz_r.at[f, 1])

        x_copy(n, 0, 1).start()
        x_copy(n, 1, 0).start()
        x_copy(n, 0, 0).start()
        x_copy(n, 1, 1).start()
        c_copy(n, 0).start()

    def stage1(n):
        arrived(n, 3, 1)
        f_copy(n, 1).start()
        arrived(n, 1, 0)
        f_copy(n, 0).start()
        arrived(n, 3, 0)
        c_copy(n, 3).start()
        arrived(n, 1, 1)
        c_copy(n, 1).start()

    def stage2(n):
        arrived(n, 2, 0)
        arrived(n, 2, 1)
        c_copy(n, 2).start()

    def block(b, fq, keys, values, biases):
        q = qb[b, fq]
        s = lax.dot_general(q, keys, (((1,), (1,)), ((), ())), preferred_element_type=F32)
        before = top[b, fq]
        peak = before
        count = len(biases)
        for n in range(count):
            part = s[:, n * CELLS : (n + 1) * CELLS]
            peak = jnp.maximum(peak, jnp.max(part, axis=1, keepdims=True) + biases[n])
        factor = jnp.exp2((before - peak) * SCALE)
        total = tot[b, fq] * factor
        pieces = []
        for n in range(count):
            shift = peak - biases[n]
            for m in range(2):
                lo = n * CELLS + m * 128
                e = jnp.exp2((s[:, lo : lo + 128] - shift) * SCALE)
                total = total + e
                pieces.append(e.astype(BF))
        mixed = jnp.dot(jnp.concatenate(pieces, axis=1), values, preferred_element_type=F32)
        top[b, fq] = peak
        tot[b, fq] = total
        acc[b, fq] = acc[b, fq] * factor + mixed

    rows_of = (seq, index(z3, x, core))

    def attend(n, dx, other_core):
        dz = lax.rem(n, 4)
        cc = lax.rem(core + other_core, 2)
        u = unit(dz, dx, cc)

        @pl.when(other_core == 1)
        def _():
            received(kvb.at[u, n // 4], bc_s.at[n, dx], bc_r.at[n, dx])

        bias0 = jnp.where(keep_ref[2 * u] > 0, 0.0, FAR)
        bias1 = jnp.where(keep_ref[2 * u + 1] > 0, 0.0, FAR)
        for b in range(2):
            same = u == rows_of[b]

            @pl.when((u <= rows_of[b]) & (n < 4))
            def _():
                block(b, 0, kvb[u, 0, 0], kvb[u, 0, 1], [jnp.where(same, 0.0, bias0)])

            @pl.when((u <= rows_of[b]) & (n >= 4))
            def _():
                keys = jnp.concatenate([kvb[u, 0, 0], kvb[u, 1, 0]], axis=0)
                values = jnp.concatenate([kvb[u, 0, 1], kvb[u, 1, 1]], axis=0)
                block(b, 1, keys, values, [bias0, jnp.where(same, 0.0, bias1)])
                block(b, 0, kvb[u, 1, 0], kvb[u, 1, 1], [jnp.where(same, FAR, bias1)])

    z_out(0)
    remote(meta_ref, metag.at[3], msend.at[0], mrecv.at[0], at_y(up))
    remote(meta_ref, metag.at[1], msend.at[1], mrecv.at[1], at_y(down))
    remote(meta_ref, metag.at[2], msend.at[2], mrecv.at[2], at_y(across))
    remote(gain_ref, gaing.at[1], gsend, grecv, at_z(4))
    own_y(0)
    relay(0)
    z_out(1)
    forward_y(0, 0)
    own_y(1)
    for n, rel in enumerate((3, 1, 2)):
        received(metag.at[rel], msend.at[n], mrecv.at[n])
    for load in loads:
        load.wait()
    relay(1)
    build_mixing(0)
    forward_y(0, 1)
    partner(0)
    build_mixing(1)
    rest_y(0, 0)
    pool(0, 0)
    forward_y(1, 0)
    rest_y(0, 1)
    pool(0, 1)
    received(gaing.at[1], gsend, grecv)
    partner(1)
    rest_y(1, 0)
    pool(1, 0)
    project(0)
    issue_own(0)
    forward_y(1, 1)

    @pl.loop(0, 11)
    def _(it):
        @pl.when(it < 8)
        def _():
            stage0(it)

        @pl.when((it >= 1) & (it < 9))
        def _():
            stage1(it - 1)

        @pl.when((it >= 2) & (it < 10))
        def _():
            stage2(it - 2)

        @pl.when(it == A_AT)
        def _():
            rest_y(1, 1)
            pool(1, 1)
            project(1)
            issue_own(1)

        @pl.loop(0, 8)
        def _(j):
            n = it - 1 - (j + 5) // 8 - (j + 1) // 8
            m = lax.rem(j, 4)
            dx = m + m // 2 - (m // 3) * 2

            @pl.when((n >= 0) & (n < 8))
            def _():
                attend(n, dx, (j + 4) // 8)

    def target(device, b):
        zz = device // 8
        row = flip(zz, b) * 8 + lax.rem(device, 8)
        return row, zz // 2

    def push(d, b):
        peer = lax.rem(seq + d, 32)
        row, h = target(seq, b)
        return describe(
            ob.at[b, peer], r_ref.at[row, h], d_s.at[b, d], d_r.at[b, d], (peer, cam, tp)
        )

    local_out = []
    for b in range(2):
        outs = []
        for f in range(2):
            total = jnp.sum(tot[b, f], axis=1, keepdims=True)
            outs.append((acc[b, f] / total).reshape(32, 8, HD))
        ob[b] = jnp.concatenate(outs, axis=1).astype(BF)

        @pl.loop(1, 32)
        def _(d):
            push(d, b).start()

        row, h = target(seq, b)
        copy = pltpu.make_async_copy(ob.at[b, seq], r_ref.at[row, h], ld.at[b])
        copy.start()
        local_out.append(copy)

    for copy in sent:
        copy.wait_send()

    @pl.loop(0, 8)
    def _(n):
        for kv in range(2):
            for toward in range(2):
                x_copy(n, toward, kv).wait_send()
            f_copy(n, kv).wait_send()
        for dx in range(4):
            c_copy(n, dx).wait_send()

    for f in range(2):
        z_copy(f).wait_send()
        for copy in own_copies(f):
            copy.wait_send()

    for b in range(2):
        @pl.loop(1, 32)
        def _(d):
            source = lax.rem(seq + 32 - d, 32)
            row, h = target(source, b)
            received(r_ref.at[row, h], d_s.at[b, d], d_r.at[b, d])

        @pl.loop(1, 32)
        def _(d):
            push(d, b).wait_send()

    for copy in local_out:
        copy.wait()


A_AT = 3
VMEM = pl.BlockSpec(memory_space=pltpu.VMEM)
ANY = pl.BlockSpec(memory_space=pl.ANY)
SMEM = pl.BlockSpec(memory_space=pltpu.SMEM)
DMA = pltpu.SemaphoreType.DMA
LIMIT = 60 * 1024 * 1024


def call_fused(x, meta, gain, keep, wq, wk, wv):
    return pl.pallas_call(
        fused,
        out_shape=jax.ShapeDtypeStruct((32, 2, 16, HD), BF),
        in_specs=[VMEM, VMEM, VMEM, SMEM, ANY, ANY, ANY],
        out_specs=VMEM,
        scratch_shapes=[
            pltpu.VMEM((2, 2, 4, 128, HALF), BF),
            pltpu.VMEM((4, 8, PIX), F32),
            pltpu.VMEM((2, 1, HALF), F32),
            pltpu.VMEM((2, ROWS, HALF), BF),
            pltpu.VMEM((2, ROWS, HALF), BF),
            pltpu.VMEM((3, D, 2 * HD), BF),
            pltpu.VMEM((2, 2, CELLS, HALF), F32),
            pltpu.VMEM((2, CELLS, HALF), BF),
            pltpu.VMEM((2, 2, CELLS, 512), BF),
            pltpu.VMEM((32, 2, 2, CELLS, HD), BF),
            pltpu.VMEM((2, 2, 2, CELLS, HD), BF),
            pltpu.VMEM((3, 2, CELLS, HD), BF),
            pltpu.VMEM((2, 2, CELLS, HD), F32),
            pltpu.VMEM((2, 2, CELLS, HD), F32),
            pltpu.VMEM((2, 2, CELLS, HD), F32),
            pltpu.VMEM((2, 32, 16, HD), BF),
            DMA((2, 2, 4)), DMA((2, 4, 4)), DMA((4,)), DMA((4,)), DMA((4,)), DMA((4,)),
            DMA((2, 4)), DMA((3,)), DMA((3,)), DMA, DMA, DMA((7,)),
            DMA((2,)), DMA((2,)), DMA((2,)), DMA((2,)), DMA((2, 2)), DMA((2, 2)),
            DMA((8, 2, 2)), DMA((8, 4, 2)), DMA((8, 2)), DMA((8, 4)), DMA((8, 4)), DMA((2,)),
            DMA((2, 32)), DMA((2, 32)), DMA((2,)),
        ],
        compiler_params=pltpu.CompilerParams(
            collective_id=0, has_side_effects=True, vmem_limit_bytes=LIMIT
        ),
        name="fused",
    )(x, meta, gain, keep, wq, wk, wv)


def local(
    pixel_feature, depth_score, depth_bin, cell_owner, cell_local, frame_keep, norm_gain,
    w_query, w_key, w_value,
):
    prob = depth_score / jnp.sum(depth_score, axis=1, keepdims=True)
    bins = jnp.arange(depth_score.shape[1], dtype=jnp.int32)
    picked = jnp.sum(
        jnp.where(depth_bin[:, :, None] == bins[None, None, :], prob[:, None, :], 0.0), axis=2
    )
    weight = lax.reduce_precision(picked, 8, 7)
    cell = (cell_owner.reshape(PIX, 4) * 8 + cell_local).astype(F32)
    meta = jnp.concatenate([weight, cell], axis=1).T
    r = call_fused(
        pixel_feature.reshape(2, 128, HALF), meta, norm_gain.reshape(1, HALF), frame_keep,
        w_query, w_key, w_value,
    )
    r = r.reshape(32, 2, 2, 8, HD)
    out = r.transpose(3, 0, 2, 1, 4)
    return out.reshape(TOK, 2 * HD)


def solution(mesh):
    return jax.shard_map(
        local,
        mesh=mesh,
        in_specs=(
            P(("seq", "cam"), "tp"),
            P(("seq", "cam"), None),
            P(("seq", "cam"), None),
            P(("seq", "cam"), None),
            P(("seq", "cam"), None),
            P(),
            P("tp"),
            P(None, ("cam", "tp")),
            P(None, ("cam", "tp")),
            P(None, ("cam", "tp")),
        ),
        out_specs=P("seq", ("cam", "tp")),
        check_vma=False,
    )
```

```python
import functools
import math

import jax
import jax.numpy as jnp
from jax import lax
from jax.experimental import pallas as pl
from jax.experimental.pallas import tpu as pltpu
from jax.sharding import PartitionSpec as P

MESH = pl.DeviceIdType.MESH
D = 2048
HALF = 1024
HD = 128
EPS = 1e-05
PIX = 256
CELLS = 256
TOK = 512
CH = 4
ROWS = PIX // CH
BF = jnp.bfloat16
F32 = jnp.float32


def where_am_i():
    seq = lax.axis_index("seq")
    cam = lax.axis_index("cam")
    tp = lax.axis_index("tp")
    z_lo = seq // 8
    x = lax.rem(seq // 2, 4)
    core = lax.rem(seq, 2)
    return seq, cam, tp, z_lo, x, core


SCALE = math.log2(math.e) / math.sqrt(HD)
FAR = -1e30
START = -0.5e30


def fused(
    x_ref, meta_ref, gain_ref, keep_ref, wq_hbm, wk_hbm, wv_hbm, r_ref,
    xg, metag, gaing, ru, rd, w_s, bev, nrm, mix, kvb, kvs, qb, acc, top, tot, ob,
    xsend, xrecv, zsend, zrecv, psend, precv, fsend, msend, mrecv, gsend, grecv, lsem,
    bpre_s, bpre_r, bq_s, bq_r, bz_s, bz_r, bx_s, bx_r, bf_s, bc_s, bc_r, lc, d_s, d_r, ld,
):
    seq, cam, tp, z_lo, x, core = where_am_i()
    z = tp * 4 + z_lo
    up, down = lax.rem(cam + 1, 4), lax.rem(cam + 3, 4)
    across = lax.rem(cam + 2, 4)
    head = z_lo // 2

    def at_y(c):
        return (seq, c, tp)

    def at_z(step):
        zz = lax.rem(z + step + 8, 8)
        return (lax.rem(zz, 4) * 8 + lax.rem(seq, 8), cam, zz // 4)

    def flip(zz, dz):
        low = lax.rem(lax.rem(zz, 2) + (dz + 1) // 2, 2)
        high = lax.rem(zz // 2 + dz // 2, 2)
        return high * 2 + low

    def index(zz, xx, cc):
        return zz * 8 + xx * 2 + cc

    def plane(zz, xx, cc):
        return (index(zz, xx, cc), cam, tp)

    right, left = lax.rem(x + 1, 4), lax.rem(x + 3, 4)
    sib = 1 - core
    z3, z1 = flip(z_lo, 2), flip(z_lo, 1)

    barrier = pltpu.get_barrier_semaphore()
    peers = [at_y(up), at_y(down), at_y(across), at_z(1), at_z(-1), at_z(3), at_z(-3), at_z(4)]
    for peer in peers:
        pl.semaphore_signal(barrier, inc=1, device_id=peer, device_id_type=MESH)

    @pl.loop(1, 32)
    def _(d):
        pl.semaphore_signal(
            barrier, inc=1, device_id=(lax.rem(seq + d, 32), cam, tp), device_id_type=MESH
        )

    loads = []
    for n, w in enumerate((wq_hbm, wk_hbm, wv_hbm)):
        loads.append(pltpu.make_async_copy(w, w_s.at[n], lsem.at[n]))
    loads.append(pltpu.make_async_copy(meta_ref, metag.at[0], lsem.at[3]))
    loads.append(pltpu.make_async_copy(gain_ref, gaing.at[0], lsem.at[4]))
    for half in range(2):
        loads.append(
            pltpu.make_async_copy(x_ref.at[half], xg.at[0, half, 0], lsem.at[5 + half])
        )
    for load in loads:
        load.start()
    acc[...] = jnp.zeros(acc.shape, F32)
    tot[...] = jnp.zeros(tot.shape, F32)
    top[...] = jnp.full(top.shape, START, F32)
    pl.semaphore_wait(barrier, len(peers) + 31)

    sent = []

    def describe(src, dst, send, recv, device):
        return pltpu.make_async_remote_copy(
            src_ref=src, dst_ref=dst, send_sem=send, recv_sem=recv, device_id=device,
            device_id_type=MESH,
        )

    def remote(src, dst, send, recv, device):
        copy = describe(src, dst, send, recv, device)
        copy.start()
        sent.append(copy)

    def received(ref, send, recv):
        describe(ref, ref, send, recv, at_y(up)).wait_recv()

    def piece(ref, c):
        return ref.at[pl.ds((c % 2) * ROWS, ROWS)]

    def z_out(f):
        for e in range(2):
            c = 2 * f + e
            target = ru if e == 0 else rd
            remote(
                piece(x_ref.at[f], c), target.at[f], zsend.at[c], zrecv.at[c],
                at_z(1) if e == 0 else at_z(-1),
            )

    def relay(f):
        for e in range(2):
            c = 2 * f + e
            ref = (ru if e == 0 else rd).at[f]
            received(ref, zsend.at[c], zrecv.at[c])
            remote(
                ref, piece(xg.at[1, f, 0], c), psend.at[c], precv.at[c],
                at_z(3) if e == 0 else at_z(-3),
            )

    def spread_y(source, p, c, toward):
        rel = 3 if toward == 0 else 1
        remote(
            source, piece(xg.at[p, c // 2, rel], c), xsend.at[p, toward, c],
            xrecv.at[p, rel, c], at_y(up if toward == 0 else down),
        )

    def own_y(f):
        for e in range(2):
            for toward in range(2):
                c = 2 * f + (1 - e if toward == 0 else e)
                spread_y(piece(x_ref.at[f], c), 0, c, toward)

    def got(p, rel, c):
        received(piece(xg.at[p, c // 2, rel], c), xsend.at[p, 0, c], xrecv.at[p, rel, c])

    def forward_y(p, f):
        for rel, c in ((3, 2 * f + 1), (1, 2 * f)):
            got(p, rel, c)
            ref = piece(xg.at[p, f, rel], c)
            remote(
                ref, piece(xg.at[p, f, 2], c), fsend.at[p, c], xrecv.at[p, 2, c],
                at_y(down if rel == 1 else up),
            )

    def rest_y(p, f):
        got(p, 3, 2 * f)
        got(p, 1, 2 * f + 1)
        got(p, 2, 2 * f)
        got(p, 2, 2 * f + 1)

    def partner(f):
        for e in range(2):
            c = 2 * f + e
            received(piece(xg.at[1, f, 0], c), psend.at[c], precv.at[c])
        for e in range(2):
            for toward in range(2):
                c = 2 * f + (1 - e if toward == 0 else e)
                spread_y(piece(xg.at[1, f, 0], c), 1, c, toward)

    def build_mixing(half):
        token = lax.broadcasted_iota(jnp.int32, (CELLS, 128), 0).astype(F32)
        for rel in range(4):
            block = metag[rel][:, half * 128 : half * 128 + 128]
            total = jnp.zeros((CELLS, 128), F32)
            for k in range(4):
                hit = token == block[4 + k : 5 + k, :]
                total = total + jnp.where(hit, block[k : k + 1, :], 0.0)
            first = total.astype(BF)
            mix[half, 0, :, rel * 128 : rel * 128 + 128] = first
            mix[half, 1, :, rel * 128 : rel * 128 + 128] = (
                total - first.astype(F32)
            ).astype(BF)

    def pool(p, f):
        rows = xg[p, f].reshape(4 * 128, HALF)
        bev[p, f] = jnp.dot(mix[f, 0], rows, preferred_element_type=F32) + jnp.dot(
            mix[f, 1], rows, preferred_element_type=F32
        )

    own = pl.multiple_of(tp * HALF, HALF)
    other = pl.multiple_of((1 - tp) * HALF, HALF)
    me = seq

    def project(f):
        step = 128
        for n in range(CELLS // step):
            a = bev[0, f, n * step : (n + 1) * step, :]
            b = bev[1, f, n * step : (n + 1) * step, :]
            squares = jnp.sum(a * a + b * b, axis=1, keepdims=True)
            scale = lax.rsqrt(squares / D + EPS)
            nrm[0, n * step : (n + 1) * step, :] = (a * scale * gaing[0]).astype(BF)
            nrm[1, n * step : (n + 1) * step, :] = (b * scale * gaing[1]).astype(BF)
        for n in (1, 2, 0):
            result = jnp.dot(nrm[0], w_s[n, pl.ds(own, HALF), :], preferred_element_type=F32)
            result = result + jnp.dot(
                nrm[1], w_s[n, pl.ds(other, HALF), :], preferred_element_type=F32
            )
            for h in range(2):
                part = result[:, h * HD : (h + 1) * HD]
                mine = lax.rem(head + h, 2)
                if n == 0:
                    qb[mine * 2, f] = part.astype(BF)
                elif n == 1:
                    kvs[mine, f, 0] = part.astype(BF)
                else:
                    flat = part.T.astype(BF)
                    kvs[mine, f, 1, 0:HD, :] = flat[:, 0:HD]
                    kvs[mine, f, 1, HD : 2 * HD, :] = flat[:, HD : 2 * HD]

    def own_copies(f):
        return [
            describe(kvs.at[1, f], kvb.at[me, f], bpre_s.at[f], bpre_r.at[f], plane(z3, x, core)),
            describe(
                kvs.at[0, f], kvb.at[me, f], bz_s.at[f, 0], bz_r.at[f, 0], plane(z1, x, core)
            ),
            describe(qb.at[2, f], qb.at[1, f], bq_s.at[f], bq_r.at[f], plane(z3, x, core)),
        ]

    def issue_own(f):
        keep_copy = pltpu.make_async_copy(kvs.at[0, f], kvb.at[me, f], lc.at[f])
        keep_copy.start()
        for copy in own_copies(f):
            copy.start()
        keep_copy.wait()

    def unit(dz, dx, cc):
        return index(flip(z_lo, dz), lax.rem(x + dx, 4), cc)

    def x_copy(n, toward, kv):
        ref = kvb.at[unit(lax.rem(n, 4), 0, core), n // 4, kv]
        return describe(
            ref, ref, bx_s.at[n, toward, kv], bx_r.at[n, 3 if toward == 0 else 1, kv],
            plane(z_lo, right if toward == 0 else left, core),
        )

    def f_copy(n, kv):
        ref = kvb.at[unit(lax.rem(n, 4), 3 if kv == 1 else 1, core), n // 4, kv]
        return describe(
            ref, ref, bf_s.at[n, kv], bx_r.at[n, 2, kv],
            plane(z_lo, right if kv == 1 else left, core),
        )

    def c_copy(n, dx):
        ref = kvb.at[unit(lax.rem(n, 4), dx, core), n // 4]
        return describe(ref, ref, bc_s.at[n, dx], bc_r.at[n, dx], plane(z_lo, x, sib))

    def z_copy(f):
        ref = kvb.at[unit(2, 0, core), f]
        return describe(ref, ref, bz_s.at[f, 1], bz_r.at[f, 1], plane(z1, x, core))

    def arrived(n, rel, kv):
        ref = kvb.at[unit(lax.rem(n, 4), rel, core), n // 4, kv]
        received(ref, bx_s.at[n, 0, kv], bx_r.at[n, rel, kv])

    def stage0(n):
        f, dz = n // 4, lax.rem(n, 4)

        @pl.when(dz == 1)
        def _():
            received(kvb.at[unit(1, 0, core), f], bz_s.at[f, 0], bz_r.at[f, 0])

        @pl.when(dz == 2)
        def _():
            received(kvb.at[unit(2, 0, core), f], bpre_s.at[f], bpre_r.at[f])
            z_copy(f).start()

        @pl.when(dz == 3)
        def _():
            received(kvb.at[unit(3, 0, core), f], bz_s.at[f, 1], bz_r.at[f, 1])

        x_copy(n, 0, 1).start()
        x_copy(n, 1, 0).start()
        x_copy(n, 0, 0).start()
        x_copy(n, 1, 1).start()
        c_copy(n, 0).start()

    def stage1(n):
        arrived(n, 3, 1)
        f_copy(n, 1).start()
        arrived(n, 1, 0)
        f_copy(n, 0).start()
        arrived(n, 3, 0)
        c_copy(n, 3).start()
        arrived(n, 1, 1)
        c_copy(n, 1).start()

    def stage2(n):
        arrived(n, 2, 0)
        arrived(n, 2, 1)
        c_copy(n, 2).start()

    def blocks(*work):
        scores = [
            lax.dot_general(
                keys, qb[b, fq], (((1,), (1,)), ((), ())), preferred_element_type=F32
            )
            for b, fq, keys, _, _ in work
        ]
        done = []
        for s, (b, fq, _, values, biases) in zip(scores, work):
            before = top[b, fq]
            peak = before
            parts = [s[n * CELLS : (n + 1) * CELLS, :] for n in range(len(biases))]
            for part, bias in zip(parts, biases):
                peak = jnp.maximum(peak, jnp.max(part, axis=0, keepdims=True) + bias)
            factor = jnp.exp2((before - peak) * SCALE)
            total = tot[b, fq] * factor
            pieces = []
            for part, bias in zip(parts, biases):
                e = jnp.exp2((part - (peak - bias)) * SCALE)
                total = total + jnp.sum(e, axis=0, keepdims=True)
                pieces.append(e.astype(BF))
            mixed = jnp.dot(values, jnp.concatenate(pieces, axis=0), preferred_element_type=F32)
            done.append((peak, total, factor, mixed))
        for (peak, total, factor, mixed), (b, fq, _, _, _) in zip(done, work):
            top[b, fq] = peak
            tot[b, fq] = total
            acc[b, fq] = acc[b, fq] * factor + mixed

    def turned(u, f):
        return jnp.concatenate([kvb[u, f, 1, 0:HD, :], kvb[u, f, 1, HD : 2 * HD, :]], axis=1)

    rows_of = (seq, index(z3, x, core))

    def attend(n, dx, other_core):
        dz = lax.rem(n, 4)
        cc = lax.rem(core + other_core, 2)
        u = unit(dz, dx, cc)

        @pl.when(other_core == 1)
        def _():
            received(kvb.at[u, n // 4], bc_s.at[n, dx], bc_r.at[n, dx])

        bias0 = jnp.where(keep_ref[2 * u] > 0, 0.0, FAR)
        bias1 = jnp.where(keep_ref[2 * u + 1] > 0, 0.0, FAR)
        low, high = head, 1 - head
        low_row = jnp.minimum(rows_of[0], rows_of[1])
        high_row = jnp.maximum(rows_of[0], rows_of[1])

        def even(b, row):
            return (b, 0, kvb[u, 0, 0], turned(u, 0), [jnp.where(u == row, 0.0, bias0)])

        def odd(b, row):
            same = u == row
            keys = jnp.concatenate([kvb[u, 0, 0], kvb[u, 1, 0]], axis=0)
            values = jnp.concatenate([turned(u, 0), turned(u, 1)], axis=1)
            return [
                (b, 1, keys, values, [bias0, jnp.where(same, 0.0, bias1)]),
                (b, 0, kvb[u, 1, 0], turned(u, 1), [jnp.where(same, FAR, bias1)]),
            ]

        @pl.when((u <= low_row) & (n < 4))
        def _():
            blocks(even(low, low_row), even(high, high_row))

        @pl.when((u > low_row) & (u <= high_row) & (n < 4))
        def _():
            blocks(even(high, high_row))

        @pl.when((u <= low_row) & (n >= 4))
        def _():
            blocks(*odd(low, low_row), *odd(high, high_row))

        @pl.when((u > low_row) & (u <= high_row) & (n >= 4))
        def _():
            blocks(*odd(high, high_row))

    z_out(0)
    remote(meta_ref, metag.at[3], msend.at[0], mrecv.at[0], at_y(up))
    remote(meta_ref, metag.at[1], msend.at[1], mrecv.at[1], at_y(down))
    remote(meta_ref, metag.at[2], msend.at[2], mrecv.at[2], at_y(across))
    remote(gain_ref, gaing.at[1], gsend, grecv, at_z(4))
    own_y(0)
    relay(0)
    z_out(1)
    forward_y(0, 0)
    own_y(1)
    for n, rel in enumerate((3, 1, 2)):
        received(metag.at[rel], msend.at[n], mrecv.at[n])
    for load in loads:
        load.wait()
    relay(1)
    build_mixing(0)
    forward_y(0, 1)
    partner(0)
    build_mixing(1)
    rest_y(0, 0)
    pool(0, 0)
    forward_y(1, 0)
    rest_y(0, 1)
    pool(0, 1)
    received(gaing.at[1], gsend, grecv)
    partner(1)
    rest_y(1, 0)
    pool(1, 0)
    project(0)
    issue_own(0)
    forward_y(1, 1)
    stage0(lax.rem(seq, 1))

    @pl.loop(0, 11)
    def _(it):
        @pl.when((it >= 1) & (it < 9))
        def _():
            stage1(it - 1)

        @pl.when(it < 7)
        def _():
            stage0(it + 1)

        @pl.when((it >= 2) & (it < 10))
        def _():
            stage2(it - 2)

        @pl.when(it == A_AT)
        def _():
            rest_y(1, 1)
            pool(1, 1)
            project(1)
            issue_own(1)

        @pl.when((it == 1) | (it == 5))
        def _():
            received(qb.at[1, it // 5], bq_s.at[it // 5], bq_r.at[it // 5])

        @pl.loop(0, 8)
        def _(j):
            n = it - 1 - (j + 5) // 8 - (j + 1) // 8
            m = lax.rem(j, 4)
            dx = m + m // 2 - (m // 3) * 2

            @pl.when((n >= 0) & (n < 8))
            def _():
                attend(n, dx, (j + 4) // 8)

    def target(device, b):
        zz = device // 8
        row = flip(zz, 2 * b) * 8 + lax.rem(device, 8)
        return row, zz // 2

    def push(d, b):
        peer = lax.rem(seq + d, 32)
        row, h = target(seq, b)
        return describe(
            ob.at[b, peer], r_ref.at[row, h], d_s.at[b, d], d_r.at[b, d], (peer, cam, tp)
        )

    local_out = []
    for b in range(2):
        outs = []
        for f in range(2):
            outs.append((acc[b, f] / tot[b, f]).T.reshape(32, 8, HD))
        ob[b] = jnp.concatenate(outs, axis=1).astype(BF)

        @pl.loop(1, 32)
        def _(d):
            push(d, b).start()

        row, h = target(seq, b)
        copy = pltpu.make_async_copy(ob.at[b, seq], r_ref.at[row, h], ld.at[b])
        copy.start()
        local_out.append(copy)

    for copy in sent:
        copy.wait_send()

    @pl.loop(0, 8)
    def _(n):
        for kv in range(2):
            for toward in range(2):
                x_copy(n, toward, kv).wait_send()
            f_copy(n, kv).wait_send()
        for dx in range(4):
            c_copy(n, dx).wait_send()

    for f in range(2):
        z_copy(f).wait_send()
        for copy in own_copies(f):
            copy.wait_send()

    for b in range(2):
        @pl.loop(1, 32)
        def _(d):
            source = lax.rem(seq + 32 - d, 32)
            row, h = target(source, b)
            received(r_ref.at[row, h], d_s.at[b, d], d_r.at[b, d])

        @pl.loop(1, 32)
        def _(d):
            push(d, b).wait_send()

    for copy in local_out:
        copy.wait()


A_AT = 2
VMEM = pl.BlockSpec(memory_space=pltpu.VMEM)
ANY = pl.BlockSpec(memory_space=pl.ANY)
SMEM = pl.BlockSpec(memory_space=pltpu.SMEM)
DMA = pltpu.SemaphoreType.DMA
LIMIT = 60 * 1024 * 1024


def call_fused(x, meta, gain, keep, wq, wk, wv):
    return pl.pallas_call(
        fused,
        out_shape=jax.ShapeDtypeStruct((32, 2, 16, HD), BF),
        in_specs=[VMEM, VMEM, VMEM, SMEM, ANY, ANY, ANY],
        out_specs=VMEM,
        scratch_shapes=[
            pltpu.VMEM((2, 2, 4, 128, HALF), BF),
            pltpu.VMEM((4, 8, PIX), F32),
            pltpu.VMEM((2, 1, HALF), F32),
            pltpu.VMEM((2, ROWS, HALF), BF),
            pltpu.VMEM((2, ROWS, HALF), BF),
            pltpu.VMEM((3, D, 2 * HD), BF),
            pltpu.VMEM((2, 2, CELLS, HALF), F32),
            pltpu.VMEM((2, CELLS, HALF), BF),
            pltpu.VMEM((2, 2, CELLS, 512), BF),
            pltpu.VMEM((32, 2, 2, CELLS, HD), BF),
            pltpu.VMEM((2, 2, 2, CELLS, HD), BF),
            pltpu.VMEM((3, 2, CELLS, HD), BF),
            pltpu.VMEM((2, 2, HD, CELLS), F32),
            pltpu.VMEM((2, 2, 1, CELLS), F32),
            pltpu.VMEM((2, 2, 1, CELLS), F32),
            pltpu.VMEM((2, 32, 16, HD), BF),
            DMA((2, 2, 4)), DMA((2, 4, 4)), DMA((4,)), DMA((4,)), DMA((4,)), DMA((4,)),
            DMA((2, 4)), DMA((3,)), DMA((3,)), DMA, DMA, DMA((7,)),
            DMA((2,)), DMA((2,)), DMA((2,)), DMA((2,)), DMA((2, 2)), DMA((2, 2)),
            DMA((8, 2, 2)), DMA((8, 4, 2)), DMA((8, 2)), DMA((8, 4)), DMA((8, 4)), DMA((2,)),
            DMA((2, 32)), DMA((2, 32)), DMA((2,)),
        ],
        compiler_params=pltpu.CompilerParams(
            collective_id=0, has_side_effects=True, vmem_limit_bytes=LIMIT
        ),
        name="fused",
    )(x, meta, gain, keep, wq, wk, wv)


def local(
    pixel_feature, depth_score, depth_bin, cell_owner, cell_local, frame_keep, norm_gain,
    w_query, w_key, w_value,
):
    prob = depth_score / jnp.sum(depth_score, axis=1, keepdims=True)
    bins = jnp.arange(depth_score.shape[1], dtype=jnp.int32)
    picked = jnp.sum(
        jnp.where(depth_bin[:, :, None] == bins[None, None, :], prob[:, None, :], 0.0), axis=2
    )
    weight = lax.reduce_precision(picked, 8, 7)
    cell = (cell_owner.reshape(PIX, 4) * 8 + cell_local).astype(F32)
    meta = jnp.concatenate([weight, cell], axis=1).T
    r = call_fused(
        pixel_feature.reshape(2, 128, HALF), meta, norm_gain.reshape(1, HALF), frame_keep,
        w_query, w_key, w_value,
    )
    r = r.reshape(32, 2, 2, 8, HD)
    out = r.transpose(3, 0, 2, 1, 4)
    return out.reshape(TOK, 2 * HD)


def solution(mesh):
    return jax.shard_map(
        local,
        mesh=mesh,
        in_specs=(
            P(("seq", "cam"), "tp"),
            P(("seq", "cam"), None),
            P(("seq", "cam"), None),
            P(("seq", "cam"), None),
            P(("seq", "cam"), None),
            P(),
            P("tp"),
            P(None, ("cam", "tp")),
            P(None, ("cam", "tp")),
            P(None, ("cam", "tp")),
        ),
        out_specs=P("seq", ("cam", "tp")),
        check_vma=False,
    )
```

```python
import functools
import math

import jax
import jax.numpy as jnp
from jax import lax
from jax.experimental import pallas as pl
from jax.experimental.pallas import tpu as pltpu
from jax.sharding import PartitionSpec as P

MESH = pl.DeviceIdType.MESH
D = 2048
HALF = 1024
HD = 128
EPS = 1e-05
PIX = 256
CELLS = 256
TOK = 512
CH = 4
ROWS = PIX // CH
BF = jnp.bfloat16
F32 = jnp.float32


def where_am_i():
    seq = lax.axis_index("seq")
    cam = lax.axis_index("cam")
    tp = lax.axis_index("tp")
    z_lo = seq // 8
    x = lax.rem(seq // 2, 4)
    core = lax.rem(seq, 2)
    return seq, cam, tp, z_lo, x, core


SCALE = math.log2(math.e) / math.sqrt(HD)
FAR = -1e30
START = -0.5e30


def fused(
    x_ref, meta_ref, gain_ref, keep_ref, wq_hbm, wk_hbm, wv_hbm, r_ref,
    xg, metag, gaing, ru, rd, w_s, bev, nrm, mix, kvb, kvs, qb, acc, top, tot, ob,
    xsend, xrecv, zsend, zrecv, psend, precv, fsend, msend, mrecv, gsend, grecv, lsem,
    bpre_s, bpre_r, bq_s, bq_r, bz_s, bz_r, bx_s, bx_r, bf_s, bc_s, bc_r, lc, d_s, d_r,
):
    seq, cam, tp, z_lo, x, core = where_am_i()
    z = tp * 4 + z_lo
    up, down = lax.rem(cam + 1, 4), lax.rem(cam + 3, 4)
    across = lax.rem(cam + 2, 4)
    head = z_lo // 2

    def at_y(c):
        return (seq, c, tp)

    def at_z(step):
        zz = lax.rem(z + step + 8, 8)
        return (lax.rem(zz, 4) * 8 + lax.rem(seq, 8), cam, zz // 4)

    def flip(zz, dz):
        low = lax.rem(lax.rem(zz, 2) + (dz + 1) // 2, 2)
        high = lax.rem(zz // 2 + dz // 2, 2)
        return high * 2 + low

    def index(zz, xx, cc):
        return zz * 8 + xx * 2 + cc

    def plane(zz, xx, cc):
        return (index(zz, xx, cc), cam, tp)

    right, left = lax.rem(x + 1, 4), lax.rem(x + 3, 4)
    sib = 1 - core
    z3, z1 = flip(z_lo, 2), flip(z_lo, 1)

    barrier = pltpu.get_barrier_semaphore()
    peers = [at_y(up), at_y(down), at_y(across), at_z(1), at_z(-1), at_z(3), at_z(-3), at_z(4)]
    for peer in peers:
        pl.semaphore_signal(barrier, inc=1, device_id=peer, device_id_type=MESH)

    @pl.loop(1, 32)
    def _(d):
        pl.semaphore_signal(
            barrier, inc=1, device_id=(lax.rem(seq + d, 32), cam, tp), device_id_type=MESH
        )

    loads = []
    for n, w in enumerate((wq_hbm, wk_hbm, wv_hbm)):
        loads.append(pltpu.make_async_copy(w, w_s.at[n], lsem.at[n]))
    loads.append(pltpu.make_async_copy(meta_ref, metag.at[0], lsem.at[3]))
    loads.append(pltpu.make_async_copy(gain_ref, gaing.at[0], lsem.at[4]))
    for half in range(2):
        loads.append(
            pltpu.make_async_copy(x_ref.at[half], xg.at[0, half, 0], lsem.at[5 + half])
        )
    for load in loads:
        load.start()
    acc[...] = jnp.zeros(acc.shape, F32)
    tot[...] = jnp.zeros(tot.shape, F32)
    top[...] = jnp.full(top.shape, START, F32)
    pl.semaphore_wait(barrier, len(peers) + 31)

    sent = []

    def describe(src, dst, send, recv, device):
        return pltpu.make_async_remote_copy(
            src_ref=src, dst_ref=dst, send_sem=send, recv_sem=recv, device_id=device,
            device_id_type=MESH,
        )

    def remote(src, dst, send, recv, device):
        copy = describe(src, dst, send, recv, device)
        copy.start()
        sent.append(copy)

    def received(ref, send, recv):
        describe(ref, ref, send, recv, at_y(up)).wait_recv()

    def piece(ref, c):
        return ref.at[pl.ds((c % 2) * ROWS, ROWS)]

    def z_out(f):
        for e in range(2):
            c = 2 * f + e
            target = ru if e == 0 else rd
            remote(
                piece(x_ref.at[f], c), target.at[f], zsend.at[c], zrecv.at[c],
                at_z(1) if e == 0 else at_z(-1),
            )

    def relay(f):
        for e in range(2):
            c = 2 * f + e
            ref = (ru if e == 0 else rd).at[f]
            received(ref, zsend.at[c], zrecv.at[c])
            remote(
                ref, piece(xg.at[1, f, 0], c), psend.at[c], precv.at[c],
                at_z(3) if e == 0 else at_z(-3),
            )

    def spread_y(source, p, c, toward):
        rel = 3 if toward == 0 else 1
        remote(
            source, piece(xg.at[p, c // 2, rel], c), xsend.at[p, toward, c],
            xrecv.at[p, rel, c], at_y(up if toward == 0 else down),
        )

    def own_y(f):
        for e in range(2):
            for toward in range(2):
                c = 2 * f + (1 - e if toward == 0 else e)
                spread_y(piece(x_ref.at[f], c), 0, c, toward)

    def got(p, rel, c):
        received(piece(xg.at[p, c // 2, rel], c), xsend.at[p, 0, c], xrecv.at[p, rel, c])

    def forward_y(p, f):
        for rel, c in ((3, 2 * f + 1), (1, 2 * f)):
            got(p, rel, c)
            ref = piece(xg.at[p, f, rel], c)
            remote(
                ref, piece(xg.at[p, f, 2], c), fsend.at[p, c], xrecv.at[p, 2, c],
                at_y(down if rel == 1 else up),
            )

    def rest_y(p, f):
        got(p, 3, 2 * f)
        got(p, 1, 2 * f + 1)
        got(p, 2, 2 * f)
        got(p, 2, 2 * f + 1)

    def partner(f):
        for e in range(2):
            c = 2 * f + e
            received(piece(xg.at[1, f, 0], c), psend.at[c], precv.at[c])
        for e in range(2):
            for toward in range(2):
                c = 2 * f + (1 - e if toward == 0 else e)
                spread_y(piece(xg.at[1, f, 0], c), 1, c, toward)

    def build_mixing(half):
        token = lax.broadcasted_iota(jnp.int32, (CELLS, 128), 0).astype(F32)
        for rel in range(4):
            block = metag[rel][:, half * 128 : half * 128 + 128]
            total = jnp.zeros((CELLS, 128), F32)
            for k in range(4):
                hit = token == block[4 + k : 5 + k, :]
                total = total + jnp.where(hit, block[k : k + 1, :], 0.0)
            first = total.astype(BF)
            mix[half, 0, :, rel * 128 : rel * 128 + 128] = first
            mix[half, 1, :, rel * 128 : rel * 128 + 128] = (
                total - first.astype(F32)
            ).astype(BF)

    def pool(p, f):
        rows = xg[p, f].reshape(4 * 128, HALF)
        bev[p, f] = jnp.dot(mix[f, 0], rows, preferred_element_type=F32) + jnp.dot(
            mix[f, 1], rows, preferred_element_type=F32
        )

    own = pl.multiple_of(tp * HALF, HALF)
    other = pl.multiple_of((1 - tp) * HALF, HALF)
    me = seq

    def project(f):
        step = 128
        for n in range(CELLS // step):
            a = bev[0, f, n * step : (n + 1) * step, :]
            b = bev[1, f, n * step : (n + 1) * step, :]
            squares = jnp.sum(a * a + b * b, axis=1, keepdims=True)
            scale = lax.rsqrt(squares / D + EPS)
            nrm[0, n * step : (n + 1) * step, :] = (a * scale * gaing[0]).astype(BF)
            nrm[1, n * step : (n + 1) * step, :] = (b * scale * gaing[1]).astype(BF)
        for n in (1, 2, 0):
            result = jnp.dot(nrm[0], w_s[n, pl.ds(own, HALF), :], preferred_element_type=F32)
            result = result + jnp.dot(
                nrm[1], w_s[n, pl.ds(other, HALF), :], preferred_element_type=F32
            )
            for h in range(2):
                part = result[:, h * HD : (h + 1) * HD]
                mine = lax.rem(head + h, 2)
                if n == 0:
                    qb[mine * 2, f] = part.astype(BF)
                elif n == 1:
                    kvs[mine, f, 0] = part.astype(BF)
                else:
                    flat = part.T.astype(BF)
                    kvs[mine, f, 1, 0:HD, :] = flat[:, 0:HD]
                    kvs[mine, f, 1, HD : 2 * HD, :] = flat[:, HD : 2 * HD]

    def own_copies(f):
        return [
            describe(kvs.at[1, f], kvb.at[me, f], bpre_s.at[f], bpre_r.at[f], plane(z3, x, core)),
            describe(
                kvs.at[0, f], kvb.at[me, f], bz_s.at[f, 0], bz_r.at[f, 0], plane(z1, x, core)
            ),
            describe(qb.at[2, f], qb.at[1, f], bq_s.at[f], bq_r.at[f], (31 - seq, cam, tp)),
        ]

    def issue_own(f):
        keep_copy = pltpu.make_async_copy(kvs.at[0, f], kvb.at[me, f], lc.at[f])
        keep_copy.start()
        for copy in own_copies(f):
            copy.start()
        keep_copy.wait()

    def unit(dz, dx, cc):
        return index(flip(z_lo, dz), lax.rem(x + dx, 4), cc)

    def x_copy(n, toward, kv):
        ref = kvb.at[unit(lax.rem(n, 4), 0, core), n // 4, kv]
        return describe(
            ref, ref, bx_s.at[n, toward, kv], bx_r.at[n, 3 if toward == 0 else 1, kv],
            plane(z_lo, right if toward == 0 else left, core),
        )

    def f_copy(n, kv):
        ref = kvb.at[unit(lax.rem(n, 4), 3 if kv == 1 else 1, core), n // 4, kv]
        return describe(
            ref, ref, bf_s.at[n, kv], bx_r.at[n, 2, kv],
            plane(z_lo, right if kv == 1 else left, core),
        )

    def c_copy(n, dx):
        ref = kvb.at[unit(lax.rem(n, 4), dx, core), n // 4]
        return describe(ref, ref, bc_s.at[n, dx], bc_r.at[n, dx], plane(z_lo, x, sib))

    def z_copy(f):
        ref = kvb.at[unit(2, 0, core), f]
        return describe(ref, ref, bz_s.at[f, 1], bz_r.at[f, 1], plane(z1, x, core))

    def arrived(n, rel, kv):
        ref = kvb.at[unit(lax.rem(n, 4), rel, core), n // 4, kv]
        received(ref, bx_s.at[n, 0, kv], bx_r.at[n, rel, kv])

    def stage0(n):
        f, dz = n // 4, lax.rem(n, 4)

        @pl.when(dz == 1)
        def _():
            received(kvb.at[unit(1, 0, core), f], bz_s.at[f, 0], bz_r.at[f, 0])

        @pl.when(dz == 2)
        def _():
            received(kvb.at[unit(2, 0, core), f], bpre_s.at[f], bpre_r.at[f])
            z_copy(f).start()

        @pl.when(dz == 3)
        def _():
            received(kvb.at[unit(3, 0, core), f], bz_s.at[f, 1], bz_r.at[f, 1])

        x_copy(n, 0, 1).start()
        x_copy(n, 1, 0).start()
        x_copy(n, 0, 0).start()
        x_copy(n, 1, 1).start()
        c_copy(n, 0).start()

    def stage1(n):
        arrived(n, 3, 1)
        f_copy(n, 1).start()
        arrived(n, 1, 0)
        f_copy(n, 0).start()
        arrived(n, 3, 0)
        c_copy(n, 3).start()
        arrived(n, 1, 1)
        c_copy(n, 1).start()

    def stage2(n):
        arrived(n, 2, 0)
        arrived(n, 2, 1)
        c_copy(n, 2).start()

    def blocks(*work):
        scores = [
            lax.dot_general(
                keys, qb[b, fq], (((1,), (1,)), ((), ())), preferred_element_type=F32
            )
            for b, fq, keys, _, _ in work
        ]
        done = []
        for s, (b, fq, _, values, biases) in zip(scores, work):
            before = top[b, fq]
            peak = before
            parts = [s[n * CELLS : (n + 1) * CELLS, :] for n in range(len(biases))]
            for part, bias in zip(parts, biases):
                peak = jnp.maximum(peak, jnp.max(part, axis=0, keepdims=True) + bias)
            factor = jnp.exp2((before - peak) * SCALE)
            total = tot[b, fq] * factor
            pieces = []
            for part, bias in zip(parts, biases):
                e = jnp.exp2((part - (peak - bias)) * SCALE)
                total = total + jnp.sum(e, axis=0, keepdims=True)
                pieces.append(e.astype(BF))
            mixed = jnp.dot(values, jnp.concatenate(pieces, axis=0), preferred_element_type=F32)
            done.append((peak, total, factor, mixed))
        for (peak, total, factor, mixed), (b, fq, _, _, _) in zip(done, work):
            top[b, fq] = peak
            tot[b, fq] = total
            acc[b, fq] = acc[b, fq] * factor + mixed

    def turned(u, f):
        return jnp.concatenate([kvb[u, f, 1, 0:HD, :], kvb[u, f, 1, HD : 2 * HD, :]], axis=1)

    rows_of = (seq, 31 - seq)

    def attend(n, dx, other_core):
        dz = lax.rem(n, 4)
        cc = lax.rem(core + other_core, 2)
        u = unit(dz, dx, cc)

        @pl.when(other_core == 1)
        def _():
            received(kvb.at[u, n // 4], bc_s.at[n, dx], bc_r.at[n, dx])

        bias0 = jnp.where(keep_ref[2 * u] > 0, 0.0, FAR)
        bias1 = jnp.where(keep_ref[2 * u + 1] > 0, 0.0, FAR)
        low, high = head, 1 - head
        low_row = jnp.minimum(rows_of[0], rows_of[1])
        high_row = jnp.maximum(rows_of[0], rows_of[1])

        def even(b, row):
            return (b, 0, kvb[u, 0, 0], turned(u, 0), [jnp.where(u == row, 0.0, bias0)])

        def odd(b, row):
            same = u == row
            keys = jnp.concatenate([kvb[u, 0, 0], kvb[u, 1, 0]], axis=0)
            values = jnp.concatenate([turned(u, 0), turned(u, 1)], axis=1)
            return [
                (b, 1, keys, values, [bias0, jnp.where(same, 0.0, bias1)]),
                (b, 0, kvb[u, 1, 0], turned(u, 1), [jnp.where(same, FAR, bias1)]),
            ]

        @pl.when((u <= low_row) & (n < 4))
        def _():
            blocks(even(low, low_row), even(high, high_row))

        @pl.when((u > low_row) & (u <= high_row) & (n < 4))
        def _():
            blocks(even(high, high_row))

        @pl.when((u <= low_row) & (n >= 4))
        def _():
            blocks(*odd(low, low_row), *odd(high, high_row))

        @pl.when((u > low_row) & (u <= high_row) & (n >= 4))
        def _():
            blocks(*odd(high, high_row))

    z_out(0)
    remote(meta_ref, metag.at[3], msend.at[0], mrecv.at[0], at_y(up))
    remote(meta_ref, metag.at[1], msend.at[1], mrecv.at[1], at_y(down))
    remote(meta_ref, metag.at[2], msend.at[2], mrecv.at[2], at_y(across))
    remote(gain_ref, gaing.at[1], gsend, grecv, at_z(4))
    own_y(0)
    relay(0)
    z_out(1)
    forward_y(0, 0)
    own_y(1)
    for n, rel in enumerate((3, 1, 2)):
        received(metag.at[rel], msend.at[n], mrecv.at[n])
    for load in loads:
        load.wait()
    relay(1)
    build_mixing(0)
    forward_y(0, 1)
    partner(0)
    build_mixing(1)
    rest_y(0, 0)
    pool(0, 0)
    forward_y(1, 0)
    rest_y(0, 1)
    pool(0, 1)
    received(gaing.at[1], gsend, grecv)
    partner(1)
    rest_y(1, 0)
    pool(1, 0)
    project(0)
    issue_own(0)
    forward_y(1, 1)
    stage0(lax.rem(seq, 1))

    @pl.loop(0, 11)
    def _(it):
        @pl.when((it >= 1) & (it < 9))
        def _():
            stage1(it - 1)

        @pl.when(it < 7)
        def _():
            stage0(it + 1)

        @pl.when((it >= 2) & (it < 10))
        def _():
            stage2(it - 2)

        @pl.when(it == A_AT)
        def _():
            rest_y(1, 1)
            pool(1, 1)
            project(1)
            issue_own(1)

        @pl.when((it == 1) | (it == 5))
        def _():
            received(qb.at[1, it // 5], bq_s.at[it // 5], bq_r.at[it // 5])

        @pl.loop(0, 8)
        def _(j):
            n = it - 1 - (j + 5) // 8 - (j + 1) // 8
            m = lax.rem(j, 4)
            dx = m + m // 2 - (m // 3) * 2

            @pl.when((n >= 0) & (n < 8))
            def _():
                attend(n, dx, (j + 4) // 8)

    def target(device, b):
        return (31 - device if b else device), device // 16

    def push(d, b):
        peer = lax.rem(seq + d, 32)
        row, h = target(seq, b)
        return describe(ob.at[b, peer], r_ref.at[row, h], d_s, d_r, (peer, cam, tp))

    for b in range(2):
        outs = []
        for f in range(2):
            outs.append((acc[b, f] / tot[b, f]).T.reshape(32, 8, HD))
        ob[b] = jnp.concatenate(outs, axis=1).astype(BF)

        @pl.loop(1, 32)
        def _(d):
            push(d, b).start()

        row, h = target(seq, b)
        pltpu.make_async_copy(ob.at[b, seq], r_ref.at[row, h], d_r).start()

    for copy in sent:
        copy.wait_send()

    @pl.loop(0, 8)
    def _(n):
        for kv in range(2):
            for toward in range(2):
                x_copy(n, toward, kv).wait_send()
            f_copy(n, kv).wait_send()
        for dx in range(4):
            c_copy(n, dx).wait_send()

    for f in range(2):
        z_copy(f).wait_send()
        for copy in own_copies(f):
            copy.wait_send()

    gone = ob.at[:, pl.ds(0, 31)]
    pltpu.make_async_copy(gone, gone, d_s).wait()
    pltpu.make_async_copy(r_ref, r_ref, d_r).wait()


A_AT = 2
VMEM = pl.BlockSpec(memory_space=pltpu.VMEM)
ANY = pl.BlockSpec(memory_space=pl.ANY)
SMEM = pl.BlockSpec(memory_space=pltpu.SMEM)
DMA = pltpu.SemaphoreType.DMA
LIMIT = 60 * 1024 * 1024


def call_fused(x, meta, gain, keep, wq, wk, wv):
    return pl.pallas_call(
        fused,
        out_shape=jax.ShapeDtypeStruct((32, 2, 16, HD), BF),
        in_specs=[VMEM, VMEM, VMEM, SMEM, ANY, ANY, ANY],
        out_specs=VMEM,
        scratch_shapes=[
            pltpu.VMEM((2, 2, 4, 128, HALF), BF),
            pltpu.VMEM((4, 8, PIX), F32),
            pltpu.VMEM((2, 1, HALF), F32),
            pltpu.VMEM((2, ROWS, HALF), BF),
            pltpu.VMEM((2, ROWS, HALF), BF),
            pltpu.VMEM((3, D, 2 * HD), BF),
            pltpu.VMEM((2, 2, CELLS, HALF), F32),
            pltpu.VMEM((2, CELLS, HALF), BF),
            pltpu.VMEM((2, 2, CELLS, 512), BF),
            pltpu.VMEM((32, 2, 2, CELLS, HD), BF),
            pltpu.VMEM((2, 2, 2, CELLS, HD), BF),
            pltpu.VMEM((3, 2, CELLS, HD), BF),
            pltpu.VMEM((2, 2, HD, CELLS), F32),
            pltpu.VMEM((2, 2, 1, CELLS), F32),
            pltpu.VMEM((2, 2, 1, CELLS), F32),
            pltpu.VMEM((2, 32, 16, HD), BF),
            DMA((2, 2, 4)), DMA((2, 4, 4)), DMA((4,)), DMA((4,)), DMA((4,)), DMA((4,)),
            DMA((2, 4)), DMA((3,)), DMA((3,)), DMA, DMA, DMA((7,)),
            DMA((2,)), DMA((2,)), DMA((2,)), DMA((2,)), DMA((2, 2)), DMA((2, 2)),
            DMA((8, 2, 2)), DMA((8, 4, 2)), DMA((8, 2)), DMA((8, 4)), DMA((8, 4)), DMA((2,)),
            DMA, DMA,
        ],
        compiler_params=pltpu.CompilerParams(
            collective_id=0, has_side_effects=True, vmem_limit_bytes=LIMIT
        ),
        name="fused",
    )(x, meta, gain, keep, wq, wk, wv)


def local(
    pixel_feature, depth_score, depth_bin, cell_owner, cell_local, frame_keep, norm_gain,
    w_query, w_key, w_value,
):
    prob = depth_score / jnp.sum(depth_score, axis=1, keepdims=True)
    bins = jnp.arange(depth_score.shape[1], dtype=jnp.int32)
    picked = jnp.sum(
        jnp.where(depth_bin[:, :, None] == bins[None, None, :], prob[:, None, :], 0.0), axis=2
    )
    weight = lax.reduce_precision(picked, 8, 7)
    cell = (cell_owner.reshape(PIX, 4) * 8 + cell_local).astype(F32)
    meta = jnp.concatenate([weight, cell], axis=1).T
    r = call_fused(
        pixel_feature.reshape(2, 128, HALF), meta, norm_gain.reshape(1, HALF), frame_keep,
        w_query, w_key, w_value,
    )
    r = r.reshape(32, 2, 2, 8, HD)
    out = r.transpose(3, 0, 2, 1, 4)
    return out.reshape(TOK, 2 * HD)


def solution(mesh):
    return jax.shard_map(
        local,
        mesh=mesh,
        in_specs=(
            P(("seq", "cam"), "tp"),
            P(("seq", "cam"), None),
            P(("seq", "cam"), None),
            P(("seq", "cam"), None),
            P(("seq", "cam"), None),
            P(),
            P("tp"),
            P(None, ("cam", "tp")),
            P(None, ("cam", "tp")),
            P(None, ("cam", "tp")),
        ),
        out_specs=P("seq", ("cam", "tp")),
        check_vma=False,
    )
```

```python
import functools
import math

import jax
import jax.numpy as jnp
from jax import lax
from jax.experimental import pallas as pl
from jax.experimental.pallas import tpu as pltpu
from jax.sharding import PartitionSpec as P

MESH = pl.DeviceIdType.MESH
D = 2048
HALF = 1024
HD = 128
EPS = 1e-05
PIX = 256
CELLS = 256
TOK = 512
CH = 4
ROWS = PIX // CH
BF = jnp.bfloat16
F32 = jnp.float32


def where_am_i():
    seq = lax.axis_index("seq")
    cam = lax.axis_index("cam")
    tp = lax.axis_index("tp")
    z_lo = seq // 8
    x = lax.rem(seq // 2, 4)
    core = lax.rem(seq, 2)
    return seq, cam, tp, z_lo, x, core


SCALE = math.log2(math.e) / math.sqrt(HD)
FAR = -1e30
START = -0.5e30


def fused(
    x_ref, meta_ref, gain_ref, keep_ref, wq_hbm, wk_hbm, wv_hbm, r_ref,
    xg, metag, gaing, ru, rd, w_s, bev, nrm, mix, kvb, kvs, qb, acc, top, tot, ob,
    xsend, xrecv, zsend, zrecv, psend, precv, fsend, msend, mrecv, gsend, grecv, lsem,
    bpre_s, bpre_r, bq_s, bq_r, bz_s, bz_r, bx_s, bx_r, bf_s, bc_s, bc_r, lc, d_s, d_r,
):
    seq, cam, tp, z_lo, x, core = where_am_i()
    z = tp * 4 + z_lo
    up, down = lax.rem(cam + 1, 4), lax.rem(cam + 3, 4)
    across = lax.rem(cam + 2, 4)
    head = z_lo // 2

    def at_y(c):
        return (seq, c, tp)

    def at_z(step):
        zz = lax.rem(z + step + 8, 8)
        return (lax.rem(zz, 4) * 8 + lax.rem(seq, 8), cam, zz // 4)

    def flip(zz, dz):
        low = lax.rem(lax.rem(zz, 2) + (dz + 1) // 2, 2)
        high = lax.rem(zz // 2 + dz // 2, 2)
        return high * 2 + low

    def index(zz, xx, cc):
        return zz * 8 + xx * 2 + cc

    def plane(zz, xx, cc):
        return (index(zz, xx, cc), cam, tp)

    right, left = lax.rem(x + 1, 4), lax.rem(x + 3, 4)
    sib = 1 - core
    z3, z1 = flip(z_lo, 2), flip(z_lo, 1)

    barrier = pltpu.get_barrier_semaphore()
    peers = [at_y(up), at_y(down), at_y(across), at_z(1), at_z(-1), at_z(3), at_z(-3), at_z(4)]
    for peer in peers:
        pl.semaphore_signal(barrier, inc=1, device_id=peer, device_id_type=MESH)

    @pl.loop(1, 32)
    def _(d):
        pl.semaphore_signal(
            barrier, inc=1, device_id=(lax.rem(seq + d, 32), cam, tp), device_id_type=MESH
        )

    loads = []
    for n, w in enumerate((wq_hbm, wk_hbm, wv_hbm)):
        loads.append(pltpu.make_async_copy(w, w_s.at[n], lsem.at[n]))
    loads.append(pltpu.make_async_copy(meta_ref, metag.at[0], lsem.at[3]))
    loads.append(pltpu.make_async_copy(gain_ref, gaing.at[0], lsem.at[4]))
    for half in range(2):
        loads.append(
            pltpu.make_async_copy(x_ref.at[half], xg.at[0, half, 0], lsem.at[5 + half])
        )
    for load in loads:
        load.start()
    acc[...] = jnp.zeros(acc.shape, F32)
    tot[...] = jnp.zeros(tot.shape, F32)
    top[...] = jnp.full(top.shape, START, F32)
    pl.semaphore_wait(barrier, len(peers) + 31)

    sent = []

    def describe(src, dst, send, recv, device):
        return pltpu.make_async_remote_copy(
            src_ref=src, dst_ref=dst, send_sem=send, recv_sem=recv, device_id=device,
            device_id_type=MESH,
        )

    def remote(src, dst, send, recv, device):
        copy = describe(src, dst, send, recv, device)
        copy.start()
        sent.append(copy)

    def received(ref, send, recv):
        describe(ref, ref, send, recv, at_y(up)).wait_recv()

    def piece(ref, c):
        return ref.at[pl.ds((c % 2) * ROWS, ROWS)]

    def z_out(f):
        for e in range(2):
            c = 2 * f + e
            target = ru if e == 0 else rd
            remote(
                piece(x_ref.at[f], c), target.at[f], zsend.at[c], zrecv.at[c],
                at_z(1) if e == 0 else at_z(-1),
            )

    def relay(f):
        for e in range(2):
            c = 2 * f + e
            ref = (ru if e == 0 else rd).at[f]
            received(ref, zsend.at[c], zrecv.at[c])
            remote(
                ref, piece(xg.at[1, f, 0], c), psend.at[c], precv.at[c],
                at_z(3) if e == 0 else at_z(-3),
            )

    def spread_y(source, p, c, toward):
        rel = 3 if toward == 0 else 1
        remote(
            source, piece(xg.at[p, c // 2, rel], c), xsend.at[p, toward, c],
            xrecv.at[p, rel, c], at_y(up if toward == 0 else down),
        )

    def own_y(f):
        for e in range(2):
            for toward in range(2):
                c = 2 * f + (1 - e if toward == 0 else e)
                spread_y(piece(x_ref.at[f], c), 0, c, toward)

    def got(p, rel, c):
        received(piece(xg.at[p, c // 2, rel], c), xsend.at[p, 0, c], xrecv.at[p, rel, c])

    def forward_y(p, f):
        for rel, c in ((3, 2 * f + 1), (1, 2 * f)):
            got(p, rel, c)
            ref = piece(xg.at[p, f, rel], c)
            remote(
                ref, piece(xg.at[p, f, 2], c), fsend.at[p, c], xrecv.at[p, 2, c],
                at_y(down if rel == 1 else up),
            )

    def rest_y(p, f):
        got(p, 3, 2 * f)
        got(p, 1, 2 * f + 1)
        got(p, 2, 2 * f)
        got(p, 2, 2 * f + 1)

    def partner(f):
        for e in range(2):
            c = 2 * f + e
            received(piece(xg.at[1, f, 0], c), psend.at[c], precv.at[c])
        for e in range(2):
            for toward in range(2):
                c = 2 * f + (1 - e if toward == 0 else e)
                spread_y(piece(xg.at[1, f, 0], c), 1, c, toward)

    def build_mixing(half):
        token = lax.broadcasted_iota(jnp.int32, (CELLS, 128), 0).astype(F32)
        for rel in range(4):
            block = metag[rel][:, half * 128 : half * 128 + 128]
            total = jnp.zeros((CELLS, 128), F32)
            for k in range(4):
                hit = token == block[4 + k : 5 + k, :]
                total = total + jnp.where(hit, block[k : k + 1, :], 0.0)
            first = total.astype(BF)
            mix[half, 0, :, rel * 128 : rel * 128 + 128] = first
            mix[half, 1, :, rel * 128 : rel * 128 + 128] = (
                total - first.astype(F32)
            ).astype(BF)

    def pool(p, f):
        rows = xg[p, f].reshape(4 * 128, HALF)
        bev[p, f] = jnp.dot(mix[f, 0], rows, preferred_element_type=F32) + jnp.dot(
            mix[f, 1], rows, preferred_element_type=F32
        )

    own = pl.multiple_of(tp * HALF, HALF)
    other = pl.multiple_of((1 - tp) * HALF, HALF)
    me = seq

    def project(f):
        step = 128
        for n in range(CELLS // step):
            a = bev[0, f, n * step : (n + 1) * step, :]
            b = bev[1, f, n * step : (n + 1) * step, :]
            squares = jnp.sum(a * a + b * b, axis=1, keepdims=True)
            scale = lax.rsqrt(squares / D + EPS)
            nrm[0, n * step : (n + 1) * step, :] = (a * scale * gaing[0]).astype(BF)
            nrm[1, n * step : (n + 1) * step, :] = (b * scale * gaing[1]).astype(BF)
        for n in (1, 2, 0):
            result = jnp.dot(nrm[0], w_s[n, pl.ds(own, HALF), :], preferred_element_type=F32)
            result = result + jnp.dot(
                nrm[1], w_s[n, pl.ds(other, HALF), :], preferred_element_type=F32
            )
            for h in range(2):
                part = result[:, h * HD : (h + 1) * HD]
                mine = lax.rem(head + h, 2)
                if n == 0:
                    qb[mine * 2, f] = part.astype(BF)
                elif n == 1:
                    kvs[mine, f, 0] = part.astype(BF)
                else:
                    flat = part.T.astype(BF)
                    kvs[mine, f, 1, 0:HD, :] = flat[:, 0:HD]
                    kvs[mine, f, 1, HD : 2 * HD, :] = flat[:, HD : 2 * HD]

    def own_copies(f):
        return [
            describe(kvs.at[1, f], kvb.at[me, f], bpre_s.at[f], bpre_r.at[f], plane(z3, x, core)),
            describe(
                kvs.at[0, f], kvb.at[me, f], bz_s.at[f, 0], bz_r.at[f, 0], plane(z1, x, core)
            ),
            describe(qb.at[2, f], qb.at[1, f], bq_s.at[f], bq_r.at[f], (31 - seq, cam, tp)),
        ]

    def issue_own(f):
        keep_copy = pltpu.make_async_copy(kvs.at[0, f], kvb.at[me, f], lc.at[f])
        keep_copy.start()
        for copy in own_copies(f):
            copy.start()
        keep_copy.wait()

    def unit(dz, dx, cc):
        return index(flip(z_lo, dz), lax.rem(x + dx, 4), cc)

    def x_copy(n, toward, kv):
        ref = kvb.at[unit(lax.rem(n, 4), 0, core), n // 4, kv]
        return describe(
            ref, ref, bx_s.at[n, toward, kv], bx_r.at[n, 3 if toward == 0 else 1, kv],
            plane(z_lo, right if toward == 0 else left, core),
        )

    def f_copy(n, kv):
        ref = kvb.at[unit(lax.rem(n, 4), 3 if kv == 1 else 1, core), n // 4, kv]
        return describe(
            ref, ref, bf_s.at[n, kv], bx_r.at[n, 2, kv],
            plane(z_lo, right if kv == 1 else left, core),
        )

    def c_copy(n, dx):
        ref = kvb.at[unit(lax.rem(n, 4), dx, core), n // 4]
        return describe(ref, ref, bc_s.at[n, dx], bc_r.at[n, dx], plane(z_lo, x, sib))

    def z_copy(f):
        ref = kvb.at[unit(2, 0, core), f]
        return describe(ref, ref, bz_s.at[f, 1], bz_r.at[f, 1], plane(z1, x, core))

    def arrived(n, rel, kv):
        ref = kvb.at[unit(lax.rem(n, 4), rel, core), n // 4, kv]
        received(ref, bx_s.at[n, 0, kv], bx_r.at[n, rel, kv])

    def stage0(n):
        f, dz = n // 4, lax.rem(n, 4)

        @pl.when(dz == 1)
        def _():
            received(kvb.at[unit(1, 0, core), f], bz_s.at[f, 0], bz_r.at[f, 0])

        @pl.when(dz == 2)
        def _():
            received(kvb.at[unit(2, 0, core), f], bpre_s.at[f], bpre_r.at[f])
            z_copy(f).start()

        @pl.when(dz == 3)
        def _():
            received(kvb.at[unit(3, 0, core), f], bz_s.at[f, 1], bz_r.at[f, 1])

        x_copy(n, 0, 1).start()
        x_copy(n, 1, 0).start()
        x_copy(n, 0, 0).start()
        x_copy(n, 1, 1).start()
        c_copy(n, 0).start()

    def stage1(n):
        arrived(n, 3, 1)
        f_copy(n, 1).start()
        arrived(n, 1, 0)
        f_copy(n, 0).start()
        arrived(n, 3, 0)
        c_copy(n, 3).start()
        arrived(n, 1, 1)
        c_copy(n, 1).start()

    def stage2(n):
        arrived(n, 2, 0)
        arrived(n, 2, 1)
        c_copy(n, 2).start()

    def blocks(*work):
        scores = [
            lax.dot_general(
                keys, qb[b, fq], (((1,), (1,)), ((), ())), preferred_element_type=F32
            )
            for b, fq, keys, _, _ in work
        ]
        done = []
        for s, (b, fq, _, values, biases) in zip(scores, work):
            before = top[b, fq]
            peak = before
            parts = [s[n * CELLS : (n + 1) * CELLS, :] for n in range(len(biases))]
            for part, bias in zip(parts, biases):
                peak = jnp.maximum(peak, jnp.max(part, axis=0, keepdims=True) + bias)
            factor = jnp.exp2((before - peak) * SCALE)
            total = tot[b, fq] * factor
            pieces = []
            for part, bias in zip(parts, biases):
                e = jnp.exp2((part - (peak - bias)) * SCALE)
                total = total + jnp.sum(e, axis=0, keepdims=True)
                pieces.append(e.astype(BF))
            mixed = jnp.dot(values, jnp.concatenate(pieces, axis=0), preferred_element_type=F32)
            done.append((peak, total, factor, mixed))
        for (peak, total, factor, mixed), (b, fq, _, _, _) in zip(done, work):
            top[b, fq] = peak
            tot[b, fq] = total
            acc[b, fq] = acc[b, fq] * factor + mixed

    def turned(u, f):
        return jnp.concatenate([kvb[u, f, 1, 0:HD, :], kvb[u, f, 1, HD : 2 * HD, :]], axis=1)

    rows_of = (seq, 31 - seq)

    def attend(n, dx):
        dz = lax.rem(n, 4)
        received(kvb.at[unit(dz, dx, sib), n // 4], bc_s.at[n, dx], bc_r.at[n, dx])
        u = unit(dz, dx, 0)
        kept = [jnp.where(keep_ref[2 * u + m] > 0, 0.0, FAR) for m in range(4)]
        low, high = head, 1 - head
        low_row = jnp.minimum(rows_of[0], rows_of[1])
        high_row = jnp.maximum(rows_of[0], rows_of[1])

        def bias(m, fq, row):
            ahead = 2 * u + m
            mine = 2 * row + fq
            open_key = jnp.where(ahead < mine, kept[m], FAR)
            return jnp.where(ahead == mine, 0.0, open_key)

        def even(b, row):
            keys = jnp.concatenate([kvb[u, 0, 0], kvb[u + 1, 0, 0]], axis=0)
            values = jnp.concatenate([turned(u, 0), turned(u + 1, 0)], axis=1)
            return (b, 0, keys, values, [bias(0, 0, row), bias(2, 0, row)])

        def odd(b, row):
            some = jnp.concatenate([kvb[u, 1, 0], kvb[u + 1, 1, 0]], axis=0)
            some_v = jnp.concatenate([turned(u, 1), turned(u + 1, 1)], axis=1)
            keys = jnp.concatenate([kvb[u, 0, 0], kvb[u + 1, 0, 0], some], axis=0)
            values = jnp.concatenate([turned(u, 0), turned(u + 1, 0), some_v], axis=1)
            return [
                (b, 1, keys, values, [bias(m, 1, row) for m in (0, 2, 1, 3)]),
                (b, 0, some, some_v, [bias(m, 0, row) for m in (1, 3)]),
            ]

        @pl.when((u <= low_row) & (n < 4))
        def _():
            blocks(even(low, low_row), even(high, high_row))

        @pl.when((u > low_row) & (u <= high_row) & (n < 4))
        def _():
            blocks(even(high, high_row))

        @pl.when((u <= low_row) & (n >= 4))
        def _():
            blocks(*odd(low, low_row), *odd(high, high_row))

        @pl.when((u > low_row) & (u <= high_row) & (n >= 4))
        def _():
            blocks(*odd(high, high_row))

    z_out(0)
    remote(meta_ref, metag.at[3], msend.at[0], mrecv.at[0], at_y(up))
    remote(meta_ref, metag.at[1], msend.at[1], mrecv.at[1], at_y(down))
    remote(meta_ref, metag.at[2], msend.at[2], mrecv.at[2], at_y(across))
    remote(gain_ref, gaing.at[1], gsend, grecv, at_z(4))
    own_y(0)
    relay(0)
    z_out(1)
    forward_y(0, 0)
    own_y(1)
    for n, rel in enumerate((3, 1, 2)):
        received(metag.at[rel], msend.at[n], mrecv.at[n])
    for load in loads:
        load.wait()
    relay(1)
    build_mixing(0)
    forward_y(0, 1)
    partner(0)
    build_mixing(1)
    rest_y(0, 0)
    pool(0, 0)
    forward_y(1, 0)
    rest_y(0, 1)
    pool(0, 1)
    received(gaing.at[1], gsend, grecv)
    partner(1)
    rest_y(1, 0)
    pool(1, 0)
    project(0)
    issue_own(0)
    forward_y(1, 1)
    stage0(lax.rem(seq, 1))

    @pl.loop(0, 10)
    def _(it):
        @pl.when((it >= 1) & (it < 9))
        def _():
            stage1(it - 1)

        @pl.when(it < 7)
        def _():
            stage0(it + 1)

        @pl.when((it >= 2) & (it < 10))
        def _():
            stage2(it - 2)

        @pl.when(it == A_AT)
        def _():
            rest_y(1, 1)
            pool(1, 1)
            project(1)
            issue_own(1)

        @pl.when((it == 1) | (it == 5))
        def _():
            received(qb.at[1, it // 5], bq_s.at[it // 5], bq_r.at[it // 5])

        @pl.loop(0, 4)
        def _(j):
            n = it - 1 - j // 3
            dx = lax.rem(3 * j, 4) - lax.rem(j // 2, 2) + 2 * (j // 3)

            @pl.when((n >= 0) & (n < 8))
            def _():
                attend(n, dx)

    def target(device, b):
        return (31 - device if b else device), device // 16

    def push(d, b):
        peer = lax.rem(seq + d, 32)
        row, h = target(seq, b)
        return describe(ob.at[b, peer], r_ref.at[row, h], d_s, d_r, (peer, cam, tp))

    for b in range(2):
        outs = []
        for f in range(2):
            outs.append((acc[b, f] / tot[b, f]).T.reshape(32, 8, HD))
        ob[b] = jnp.concatenate(outs, axis=1).astype(BF)

        @pl.loop(1, 32)
        def _(d):
            push(d, b).start()

        row, h = target(seq, b)
        pltpu.make_async_copy(ob.at[b, seq], r_ref.at[row, h], d_r).start()

    for copy in sent:
        copy.wait_send()

    @pl.loop(0, 8)
    def _(n):
        for kv in range(2):
            for toward in range(2):
                x_copy(n, toward, kv).wait_send()
            f_copy(n, kv).wait_send()
        for dx in range(4):
            c_copy(n, dx).wait_send()

    for f in range(2):
        z_copy(f).wait_send()
        for copy in own_copies(f):
            copy.wait_send()

    gone = ob.at[:, pl.ds(0, 31)]
    pltpu.make_async_copy(gone, gone, d_s).wait()
    pltpu.make_async_copy(r_ref, r_ref, d_r).wait()


A_AT = 2
VMEM = pl.BlockSpec(memory_space=pltpu.VMEM)
ANY = pl.BlockSpec(memory_space=pl.ANY)
SMEM = pl.BlockSpec(memory_space=pltpu.SMEM)
DMA = pltpu.SemaphoreType.DMA
LIMIT = 60 * 1024 * 1024


def call_fused(x, meta, gain, keep, wq, wk, wv):
    return pl.pallas_call(
        fused,
        out_shape=jax.ShapeDtypeStruct((32, 2, 16, HD), BF),
        in_specs=[VMEM, VMEM, VMEM, SMEM, ANY, ANY, ANY],
        out_specs=VMEM,
        scratch_shapes=[
            pltpu.VMEM((2, 2, 4, 128, HALF), BF),
            pltpu.VMEM((4, 8, PIX), F32),
            pltpu.VMEM((2, 1, HALF), F32),
            pltpu.VMEM((2, ROWS, HALF), BF),
            pltpu.VMEM((2, ROWS, HALF), BF),
            pltpu.VMEM((3, D, 2 * HD), BF),
            pltpu.VMEM((2, 2, CELLS, HALF), F32),
            pltpu.VMEM((2, CELLS, HALF), BF),
            pltpu.VMEM((2, 2, CELLS, 512), BF),
            pltpu.VMEM((32, 2, 2, CELLS, HD), BF),
            pltpu.VMEM((2, 2, 2, CELLS, HD), BF),
            pltpu.VMEM((3, 2, CELLS, HD), BF),
            pltpu.VMEM((2, 2, HD, CELLS), F32),
            pltpu.VMEM((2, 2, 1, CELLS), F32),
            pltpu.VMEM((2, 2, 1, CELLS), F32),
            pltpu.VMEM((2, 32, 16, HD), BF),
            DMA((2, 2, 4)), DMA((2, 4, 4)), DMA((4,)), DMA((4,)), DMA((4,)), DMA((4,)),
            DMA((2, 4)), DMA((3,)), DMA((3,)), DMA, DMA, DMA((7,)),
            DMA((2,)), DMA((2,)), DMA((2,)), DMA((2,)), DMA((2, 2)), DMA((2, 2)),
            DMA((8, 2, 2)), DMA((8, 4, 2)), DMA((8, 2)), DMA((8, 4)), DMA((8, 4)), DMA((2,)),
            DMA, DMA,
        ],
        compiler_params=pltpu.CompilerParams(
            collective_id=0, has_side_effects=True, vmem_limit_bytes=LIMIT
        ),
        name="fused",
    )(x, meta, gain, keep, wq, wk, wv)


def local(
    pixel_feature, depth_score, depth_bin, cell_owner, cell_local, frame_keep, norm_gain,
    w_query, w_key, w_value,
):
    prob = depth_score / jnp.sum(depth_score, axis=1, keepdims=True)
    bins = jnp.arange(depth_score.shape[1], dtype=jnp.int32)
    picked = jnp.sum(
        jnp.where(depth_bin[:, :, None] == bins[None, None, :], prob[:, None, :], 0.0), axis=2
    )
    weight = lax.reduce_precision(picked, 8, 7)
    cell = (cell_owner.reshape(PIX, 4) * 8 + cell_local).astype(F32)
    meta = jnp.concatenate([weight, cell], axis=1).T
    r = call_fused(
        pixel_feature.reshape(2, 128, HALF), meta, norm_gain.reshape(1, HALF), frame_keep,
        w_query, w_key, w_value,
    )
    r = r.reshape(32, 2, 2, 8, HD)
    out = r.transpose(3, 0, 2, 1, 4)
    return out.reshape(TOK, 2 * HD)


def solution(mesh):
    return jax.shard_map(
        local,
        mesh=mesh,
        in_specs=(
            P(("seq", "cam"), "tp"),
            P(("seq", "cam"), None),
            P(("seq", "cam"), None),
            P(("seq", "cam"), None),
            P(("seq", "cam"), None),
            P(),
            P("tp"),
            P(None, ("cam", "tp")),
            P(None, ("cam", "tp")),
            P(None, ("cam", "tp")),
        ),
        out_specs=P("seq", ("cam", "tp")),
        check_vma=False,
    )
```

```python
import functools
import math

import jax
import jax.numpy as jnp
from jax import lax
from jax.experimental import pallas as pl
from jax.experimental.pallas import tpu as pltpu
from jax.sharding import PartitionSpec as P

MESH = pl.DeviceIdType.MESH
D = 2048
HALF = 1024
HD = 128
EPS = 1e-05
PIX = 256
CELLS = 256
TOK = 512
CH = 4
ROWS = PIX // CH
BF = jnp.bfloat16
F32 = jnp.float32


def where_am_i():
    seq = lax.axis_index("seq")
    cam = lax.axis_index("cam")
    tp = lax.axis_index("tp")
    z_lo = seq // 8
    x = lax.rem(seq // 2, 4)
    core = lax.rem(seq, 2)
    return seq, cam, tp, z_lo, x, core


SCALE = math.log2(math.e) / math.sqrt(HD)
FAR = -1e30
START = -0.5e30


def fused(
    x_ref, meta_ref, gain_ref, keep_ref, wq_hbm, wk_hbm, wv_hbm, r_ref,
    xg, metag, gaing, ru, rd, w_s, bev, nrm, mix, kvb, kvs, qb, acc, top, tot, ob,
    xsend, xrecv, zsend, zrecv, psend, precv, fsend, msend, mrecv, gsend, grecv, lsem,
    bpre_s, bpre_r, bq_s, bq_r, bz_s, bz_r, bx_s, bx_r, bf_s, bc_s, bc_r, lc, d_s, d_r,
):
    seq, cam, tp, z_lo, x, core = where_am_i()
    z = tp * 4 + z_lo
    up, down = lax.rem(cam + 1, 4), lax.rem(cam + 3, 4)
    across = lax.rem(cam + 2, 4)
    head = z_lo // 2

    def at_y(c):
        return (seq, c, tp)

    def at_z(step):
        zz = lax.rem(z + step + 8, 8)
        return (lax.rem(zz, 4) * 8 + lax.rem(seq, 8), cam, zz // 4)

    def flip(zz, dz):
        low = lax.rem(lax.rem(zz, 2) + (dz + 1) // 2, 2)
        high = lax.rem(zz // 2 + dz // 2, 2)
        return high * 2 + low

    def index(zz, xx, cc):
        return zz * 8 + xx * 2 + cc

    def plane(zz, xx, cc):
        return (index(zz, xx, cc), cam, tp)

    right, left = lax.rem(x + 1, 4), lax.rem(x + 3, 4)
    sib = 1 - core
    z3, z1 = flip(z_lo, 2), flip(z_lo, 1)

    barrier = pltpu.get_barrier_semaphore()
    peers = [at_y(up), at_y(down), at_y(across), at_z(1), at_z(-1), at_z(3), at_z(-3), at_z(4)]
    for peer in peers:
        pl.semaphore_signal(barrier, inc=1, device_id=peer, device_id_type=MESH)

    @pl.loop(1, 32)
    def _(d):
        pl.semaphore_signal(
            barrier, inc=1, device_id=(lax.rem(seq + d, 32), cam, tp), device_id_type=MESH
        )

    loads = []
    for n, w in enumerate((wq_hbm, wk_hbm, wv_hbm)):
        loads.append(pltpu.make_async_copy(w, w_s.at[n], lsem.at[n]))
    loads.append(pltpu.make_async_copy(meta_ref, metag.at[0], lsem.at[3]))
    loads.append(pltpu.make_async_copy(gain_ref, gaing.at[0], lsem.at[4]))
    for half in range(2):
        loads.append(
            pltpu.make_async_copy(x_ref.at[half], xg.at[0, half, 0], lsem.at[5 + half])
        )
    for load in loads:
        load.start()
    acc[...] = jnp.zeros(acc.shape, F32)
    tot[...] = jnp.zeros(tot.shape, F32)
    top[...] = jnp.full(top.shape, START, F32)
    pl.semaphore_wait(barrier, len(peers) + 31)

    sent = []

    def describe(src, dst, send, recv, device):
        return pltpu.make_async_remote_copy(
            src_ref=src, dst_ref=dst, send_sem=send, recv_sem=recv, device_id=device,
            device_id_type=MESH,
        )

    def remote(src, dst, send, recv, device):
        copy = describe(src, dst, send, recv, device)
        copy.start()
        sent.append(copy)

    def received(ref, send, recv):
        describe(ref, ref, send, recv, at_y(up)).wait_recv()

    def piece(ref, c):
        return ref.at[pl.ds((c % 2) * ROWS, ROWS)]

    def z_out(f):
        for e in range(2):
            c = 2 * f + e
            target = ru if e == 0 else rd
            remote(
                piece(x_ref.at[f], c), target.at[f], zsend.at[c], zrecv.at[c],
                at_z(1) if e == 0 else at_z(-1),
            )

    def relay(f):
        for e in range(2):
            c = 2 * f + e
            ref = (ru if e == 0 else rd).at[f]
            received(ref, zsend.at[c], zrecv.at[c])
            remote(
                ref, piece(xg.at[1, f, 0], c), psend.at[c], precv.at[c],
                at_z(3) if e == 0 else at_z(-3),
            )

    def spread_y(source, p, c, toward):
        rel = 3 if toward == 0 else 1
        remote(
            source, piece(xg.at[p, c // 2, rel], c), xsend.at[p, toward, c],
            xrecv.at[p, rel, c], at_y(up if toward == 0 else down),
        )

    def own_y(f):
        for e in range(2):
            for toward in range(2):
                c = 2 * f + (1 - e if toward == 0 else e)
                spread_y(piece(x_ref.at[f], c), 0, c, toward)

    def got(p, rel, c):
        received(piece(xg.at[p, c // 2, rel], c), xsend.at[p, 0, c], xrecv.at[p, rel, c])

    def forward_y(p, f):
        for rel, c in ((3, 2 * f + 1), (1, 2 * f)):
            got(p, rel, c)
            ref = piece(xg.at[p, f, rel], c)
            remote(
                ref, piece(xg.at[p, f, 2], c), fsend.at[p, c], xrecv.at[p, 2, c],
                at_y(down if rel == 1 else up),
            )

    def rest_y(p, f):
        got(p, 3, 2 * f)
        got(p, 1, 2 * f + 1)
        got(p, 2, 2 * f)
        got(p, 2, 2 * f + 1)

    def partner(f):
        for e in range(2):
            c = 2 * f + e
            received(piece(xg.at[1, f, 0], c), psend.at[c], precv.at[c])
        for e in range(2):
            for toward in range(2):
                c = 2 * f + (1 - e if toward == 0 else e)
                spread_y(piece(xg.at[1, f, 0], c), 1, c, toward)

    def build_mixing(half):
        token = lax.broadcasted_iota(jnp.int32, (CELLS, 128), 0).astype(F32)
        for rel in range(4):
            block = metag[rel][:, half * 128 : half * 128 + 128]
            total = jnp.zeros((CELLS, 128), F32)
            for k in range(4):
                hit = token == block[4 + k : 5 + k, :]
                total = total + jnp.where(hit, block[k : k + 1, :], 0.0)
            first = total.astype(BF)
            mix[half, 0, :, rel * 128 : rel * 128 + 128] = first
            mix[half, 1, :, rel * 128 : rel * 128 + 128] = (
                total - first.astype(F32)
            ).astype(BF)

    def pool(p, f):
        rows = xg[p, f].reshape(4 * 128, HALF)
        bev[p, f] = jnp.dot(mix[f, 0], rows, preferred_element_type=F32) + jnp.dot(
            mix[f, 1], rows, preferred_element_type=F32
        )

    own = pl.multiple_of(tp * HALF, HALF)
    other = pl.multiple_of((1 - tp) * HALF, HALF)
    me = seq

    def project(f):
        step = 128
        for n in range(CELLS // step):
            a = bev[0, f, n * step : (n + 1) * step, :]
            b = bev[1, f, n * step : (n + 1) * step, :]
            squares = jnp.sum(a * a + b * b, axis=1, keepdims=True)
            scale = lax.rsqrt(squares / D + EPS)
            nrm[0, n * step : (n + 1) * step, :] = (a * scale * gaing[0]).astype(BF)
            nrm[1, n * step : (n + 1) * step, :] = (b * scale * gaing[1]).astype(BF)

    def multiply(f, n):
        result = jnp.dot(nrm[0], w_s[n, pl.ds(own, HALF), :], preferred_element_type=F32)
        result = result + jnp.dot(
            nrm[1], w_s[n, pl.ds(other, HALF), :], preferred_element_type=F32
        )
        for h in range(2):
            part = result[:, h * HD : (h + 1) * HD]
            mine = lax.rem(head + h, 2)
            if n == 0:
                qb[mine * 2, f] = part.astype(BF)
            elif n == 1:
                kvs[mine, f, 0] = part.astype(BF)
            else:
                flat = part.T.astype(BF)
                kvs[mine, f, 1, 0:HD, :] = flat[:, 0:HD]
                kvs[mine, f, 1, HD : 2 * HD, :] = flat[:, HD : 2 * HD]

    def own_copies(f):
        return [
            describe(kvs.at[1, f], kvb.at[me, f], bpre_s.at[f], bpre_r.at[f], plane(z3, x, core)),
            describe(
                kvs.at[0, f], kvb.at[me, f], bz_s.at[f, 0], bz_r.at[f, 0], plane(z1, x, core)
            ),
            describe(qb.at[2, f], qb.at[1, f], bq_s.at[f], bq_r.at[f], (31 - seq, cam, tp)),
        ]

    def issue_own(f):
        multiply(f, 1)
        multiply(f, 2)
        keep_copy = pltpu.make_async_copy(kvs.at[0, f], kvb.at[me, f], lc.at[f])
        keep_copy.start()
        copies = own_copies(f)
        copies[0].start()
        copies[1].start()
        keep_copy.wait()
        if f == 0:
            stage0(lax.rem(seq, 1))
        multiply(f, 0)
        copies[2].start()

    def unit(dz, dx, cc):
        return index(flip(z_lo, dz), lax.rem(x + dx, 4), cc)

    def x_copy(n, toward, kv):
        ref = kvb.at[unit(lax.rem(n, 4), 0, core), n // 4, kv]
        return describe(
            ref, ref, bx_s.at[n, toward, kv], bx_r.at[n, 3 if toward == 0 else 1, kv],
            plane(z_lo, right if toward == 0 else left, core),
        )

    def f_copy(n, kv):
        ref = kvb.at[unit(lax.rem(n, 4), 3 if kv == 1 else 1, core), n // 4, kv]
        return describe(
            ref, ref, bf_s.at[n, kv], bx_r.at[n, 2, kv],
            plane(z_lo, right if kv == 1 else left, core),
        )

    def c_copy(n, dx):
        ref = kvb.at[unit(lax.rem(n, 4), dx, core), n // 4]
        return describe(ref, ref, bc_s.at[n, dx], bc_r.at[n, dx], plane(z_lo, x, sib))

    def z_copy(f):
        ref = kvb.at[unit(2, 0, core), f]
        return describe(ref, ref, bz_s.at[f, 1], bz_r.at[f, 1], plane(z1, x, core))

    def arrived(n, rel, kv):
        ref = kvb.at[unit(lax.rem(n, 4), rel, core), n // 4, kv]
        received(ref, bx_s.at[n, 0, kv], bx_r.at[n, rel, kv])

    def stage0(n):
        f, dz = n // 4, lax.rem(n, 4)

        @pl.when(dz == 1)
        def _():
            received(kvb.at[unit(1, 0, core), f], bz_s.at[f, 0], bz_r.at[f, 0])

        @pl.when(dz == 2)
        def _():
            received(kvb.at[unit(2, 0, core), f], bpre_s.at[f], bpre_r.at[f])
            z_copy(f).start()

        @pl.when(dz == 3)
        def _():
            received(kvb.at[unit(3, 0, core), f], bz_s.at[f, 1], bz_r.at[f, 1])

        x_copy(n, 0, 1).start()
        x_copy(n, 1, 0).start()
        x_copy(n, 0, 0).start()
        x_copy(n, 1, 1).start()
        c_copy(n, 0).start()

    def stage1(n):
        arrived(n, 3, 1)
        f_copy(n, 1).start()
        arrived(n, 1, 0)
        f_copy(n, 0).start()
        arrived(n, 3, 0)
        c_copy(n, 3).start()
        arrived(n, 1, 1)
        c_copy(n, 1).start()

    def stage2(n):
        arrived(n, 2, 0)
        arrived(n, 2, 1)
        c_copy(n, 2).start()

    def blocks(*work):
        scores = [
            lax.dot_general(
                keys, qb[b, fq], (((1,), (1,)), ((), ())), preferred_element_type=F32
            )
            for b, fq, keys, _, _ in work
        ]
        done = []
        for s, (b, fq, _, values, biases) in zip(scores, work):
            before = top[b, fq]
            peak = before
            parts = [s[n * CELLS : (n + 1) * CELLS, :] for n in range(len(biases))]
            for part, bias in zip(parts, biases):
                peak = jnp.maximum(peak, jnp.max(part, axis=0, keepdims=True) + bias)
            factor = jnp.exp2((before - peak) * SCALE)
            total = tot[b, fq] * factor
            pieces = []
            for part, bias in zip(parts, biases):
                e = jnp.exp2((part - (peak - bias)) * SCALE)
                total = total + jnp.sum(e, axis=0, keepdims=True)
                pieces.append(e.astype(BF))
            mixed = jnp.dot(values, jnp.concatenate(pieces, axis=0), preferred_element_type=F32)
            done.append((peak, total, factor, mixed))
        for (peak, total, factor, mixed), (b, fq, _, _, _) in zip(done, work):
            top[b, fq] = peak
            tot[b, fq] = total
            acc[b, fq] = acc[b, fq] * factor + mixed

    def turned(u, f):
        return jnp.concatenate([kvb[u, f, 1, 0:HD, :], kvb[u, f, 1, HD : 2 * HD, :]], axis=1)

    rows_of = (seq, 31 - seq)

    def attend(n, dx):
        dz = lax.rem(n, 4)
        received(kvb.at[unit(dz, dx, sib), n // 4], bc_s.at[n, dx], bc_r.at[n, dx])
        u = unit(dz, dx, 0)
        kept = [jnp.where(keep_ref[2 * u + m] > 0, 0.0, FAR) for m in range(4)]
        low, high = head, 1 - head
        low_row = jnp.minimum(rows_of[0], rows_of[1])
        high_row = jnp.maximum(rows_of[0], rows_of[1])

        def bias(m, fq, row):
            ahead = 2 * u + m
            mine = 2 * row + fq
            open_key = jnp.where(ahead < mine, kept[m], FAR)
            return jnp.where(ahead == mine, 0.0, open_key)

        def even(b, row):
            keys = jnp.concatenate([kvb[u, 0, 0], kvb[u + 1, 0, 0]], axis=0)
            values = jnp.concatenate([turned(u, 0), turned(u + 1, 0)], axis=1)
            return (b, 0, keys, values, [bias(0, 0, row), bias(2, 0, row)])

        def odd(b, row):
            some = jnp.concatenate([kvb[u, 1, 0], kvb[u + 1, 1, 0]], axis=0)
            some_v = jnp.concatenate([turned(u, 1), turned(u + 1, 1)], axis=1)
            keys = jnp.concatenate([kvb[u, 0, 0], kvb[u + 1, 0, 0], some], axis=0)
            values = jnp.concatenate([turned(u, 0), turned(u + 1, 0), some_v], axis=1)
            return [
                (b, 1, keys, values, [bias(m, 1, row) for m in (0, 2, 1, 3)]),
                (b, 0, some, some_v, [bias(m, 0, row) for m in (1, 3)]),
            ]

        @pl.when((u <= low_row) & (n < 4))
        def _():
            blocks(even(low, low_row), even(high, high_row))

        @pl.when((u > low_row) & (u <= high_row) & (n < 4))
        def _():
            blocks(even(high, high_row))

        @pl.when((u <= low_row) & (n >= 4))
        def _():
            blocks(*odd(low, low_row), *odd(high, high_row))

        @pl.when((u > low_row) & (u <= high_row) & (n >= 4))
        def _():
            blocks(*odd(high, high_row))

    z_out(0)
    remote(meta_ref, metag.at[3], msend.at[0], mrecv.at[0], at_y(up))
    remote(meta_ref, metag.at[1], msend.at[1], mrecv.at[1], at_y(down))
    remote(meta_ref, metag.at[2], msend.at[2], mrecv.at[2], at_y(across))
    remote(gain_ref, gaing.at[1], gsend, grecv, at_z(4))
    own_y(0)
    relay(0)
    z_out(1)
    forward_y(0, 0)
    own_y(1)
    for n, rel in enumerate((3, 1, 2)):
        received(metag.at[rel], msend.at[n], mrecv.at[n])
    for load in loads:
        load.wait()
    relay(1)
    build_mixing(0)
    forward_y(0, 1)
    partner(0)
    build_mixing(1)
    rest_y(0, 0)
    pool(0, 0)
    forward_y(1, 0)
    rest_y(0, 1)
    pool(0, 1)
    received(gaing.at[1], gsend, grecv)
    partner(1)
    rest_y(1, 0)
    pool(1, 0)
    project(0)
    issue_own(0)
    forward_y(1, 1)

    @pl.loop(0, 10)
    def _(it):
        @pl.when((it >= 1) & (it < 9))
        def _():
            stage1(it - 1)

        @pl.when(it < 7)
        def _():
            stage0(it + 1)

        @pl.when((it >= 2) & (it < 10))
        def _():
            stage2(it - 2)

        @pl.when(it == A_AT)
        def _():
            rest_y(1, 1)
            pool(1, 1)
            project(1)
            issue_own(1)

        @pl.when((it == 1) | (it == 5))
        def _():
            received(qb.at[1, it // 5], bq_s.at[it // 5], bq_r.at[it // 5])

        @pl.loop(0, 4)
        def _(j):
            n = it - 1 - j // 3
            dx = lax.rem(3 * j, 4) - lax.rem(j // 2, 2) + 2 * (j // 3)

            @pl.when((n >= 0) & (n < 8))
            def _():
                attend(n, dx)

    def target(device, b):
        return (31 - device if b else device), device // 16

    def push(d, b):
        peer = lax.rem(seq + d, 32)
        row, h = target(seq, b)
        return describe(ob.at[b, peer], r_ref.at[row, h], d_s, d_r, (peer, cam, tp))

    for b in range(2):
        outs = []
        for f in range(2):
            outs.append((acc[b, f] / tot[b, f]).T.reshape(32, 8, HD))
        ob[b] = jnp.concatenate(outs, axis=1).astype(BF)

        @pl.loop(1, 32)
        def _(d):
            push(d, b).start()

        row, h = target(seq, b)
        pltpu.make_async_copy(ob.at[b, seq], r_ref.at[row, h], d_r).start()

    for copy in sent:
        copy.wait_send()

    @pl.loop(0, 8)
    def _(n):
        for kv in range(2):
            for toward in range(2):
                x_copy(n, toward, kv).wait_send()
            f_copy(n, kv).wait_send()
        for dx in range(4):
            c_copy(n, dx).wait_send()

    for f in range(2):
        z_copy(f).wait_send()
        for copy in own_copies(f):
            copy.wait_send()

    gone = ob.at[:, pl.ds(0, 31)]
    pltpu.make_async_copy(gone, gone, d_s).wait()
    pltpu.make_async_copy(r_ref, r_ref, d_r).wait()


A_AT = 2
VMEM = pl.BlockSpec(memory_space=pltpu.VMEM)
ANY = pl.BlockSpec(memory_space=pl.ANY)
SMEM = pl.BlockSpec(memory_space=pltpu.SMEM)
DMA = pltpu.SemaphoreType.DMA
LIMIT = 60 * 1024 * 1024


def call_fused(x, meta, gain, keep, wq, wk, wv):
    return pl.pallas_call(
        fused,
        out_shape=jax.ShapeDtypeStruct((32, 2, 16, HD), BF),
        in_specs=[ANY, VMEM, VMEM, SMEM, ANY, ANY, ANY],
        out_specs=VMEM,
        scratch_shapes=[
            pltpu.VMEM((2, 2, 4, 128, HALF), BF),
            pltpu.VMEM((4, 8, PIX), F32),
            pltpu.VMEM((2, 1, HALF), F32),
            pltpu.VMEM((2, ROWS, HALF), BF),
            pltpu.VMEM((2, ROWS, HALF), BF),
            pltpu.VMEM((3, D, 2 * HD), BF),
            pltpu.VMEM((2, 2, CELLS, HALF), F32),
            pltpu.VMEM((2, CELLS, HALF), BF),
            pltpu.VMEM((2, 2, CELLS, 512), BF),
            pltpu.VMEM((32, 2, 2, CELLS, HD), BF),
            pltpu.VMEM((2, 2, 2, CELLS, HD), BF),
            pltpu.VMEM((3, 2, CELLS, HD), BF),
            pltpu.VMEM((2, 2, HD, CELLS), F32),
            pltpu.VMEM((2, 2, 1, CELLS), F32),
            pltpu.VMEM((2, 2, 1, CELLS), F32),
            pltpu.VMEM((2, 32, 16, HD), BF),
            DMA((2, 2, 4)), DMA((2, 4, 4)), DMA((4,)), DMA((4,)), DMA((4,)), DMA((4,)),
            DMA((2, 4)), DMA((3,)), DMA((3,)), DMA, DMA, DMA((7,)),
            DMA((2,)), DMA((2,)), DMA((2,)), DMA((2,)), DMA((2, 2)), DMA((2, 2)),
            DMA((8, 2, 2)), DMA((8, 4, 2)), DMA((8, 2)), DMA((8, 4)), DMA((8, 4)), DMA((2,)),
            DMA, DMA,
        ],
        compiler_params=pltpu.CompilerParams(
            collective_id=0, has_side_effects=True, vmem_limit_bytes=LIMIT
        ),
        name="fused",
    )(x, meta, gain, keep, wq, wk, wv)


def local(
    pixel_feature, depth_score, depth_bin, cell_owner, cell_local, frame_keep, norm_gain,
    w_query, w_key, w_value,
):
    prob = depth_score / jnp.sum(depth_score, axis=1, keepdims=True)
    bins = jnp.arange(depth_score.shape[1], dtype=jnp.int32)
    picked = jnp.sum(
        jnp.where(depth_bin[:, :, None] == bins[None, None, :], prob[:, None, :], 0.0), axis=2
    )
    weight = lax.reduce_precision(picked, 8, 7)
    cell = (cell_owner.reshape(PIX, 4) * 8 + cell_local).astype(F32)
    meta = jnp.concatenate([weight, cell], axis=1).T
    r = call_fused(
        pixel_feature.reshape(2, 128, HALF), meta, norm_gain.reshape(1, HALF), frame_keep,
        w_query, w_key, w_value,
    )
    r = r.reshape(32, 2, 2, 8, HD)
    out = r.transpose(3, 0, 2, 1, 4)
    return out.reshape(TOK, 2 * HD)


def solution(mesh):
    return jax.shard_map(
        local,
        mesh=mesh,
        in_specs=(
            P(("seq", "cam"), "tp"),
            P(("seq", "cam"), None),
            P(("seq", "cam"), None),
            P(("seq", "cam"), None),
            P(("seq", "cam"), None),
            P(),
            P("tp"),
            P(None, ("cam", "tp")),
            P(None, ("cam", "tp")),
            P(None, ("cam", "tp")),
        ),
        out_specs=P("seq", ("cam", "tp")),
        check_vma=False,
    )
```

```python
import functools
import math

import jax
import jax.numpy as jnp
from jax import lax
from jax.experimental import pallas as pl
from jax.experimental.pallas import tpu as pltpu
from jax.sharding import PartitionSpec as P

MESH = pl.DeviceIdType.MESH
D = 2048
HALF = 1024
HD = 128
EPS = 1e-05
PIX = 256
CELLS = 256
TOK = 512
CH = 4
ROWS = PIX // CH
BF = jnp.bfloat16
F32 = jnp.float32


def where_am_i():
    seq = lax.axis_index("seq")
    cam = lax.axis_index("cam")
    tp = lax.axis_index("tp")
    z_lo = seq // 8
    x = lax.rem(seq // 2, 4)
    core = lax.rem(seq, 2)
    return seq, cam, tp, z_lo, x, core


SCALE = math.log2(math.e) / math.sqrt(HD)
FAR = -1e30
START = -0.5e30


def fused(
    x_ref, meta_ref, gain_ref, keep_ref, wq_hbm, wk_hbm, wv_hbm, r_ref,
    xg, metag, gaing, ru, rd, w_s, bev, nrm, mix, kvb, kvs, qb, acc, top, tot, ob,
    xsend, xrecv, zsend, zrecv, psend, precv, fsend, msend, mrecv, gsend, grecv, lsem,
    bpre_s, bpre_r, bq_s, bq_r, bz_s, bz_r, bx_s, bx_r, bf_s, bc_s, bc_r, lc, d_s, d_r,
):
    seq, cam, tp, z_lo, x, core = where_am_i()
    z = tp * 4 + z_lo
    up, down = lax.rem(cam + 1, 4), lax.rem(cam + 3, 4)
    across = lax.rem(cam + 2, 4)
    head = z_lo // 2

    def at_y(c):
        return (seq, c, tp)

    def at_z(step):
        zz = lax.rem(z + step + 8, 8)
        return (lax.rem(zz, 4) * 8 + lax.rem(seq, 8), cam, zz // 4)

    def flip(zz, dz):
        low = lax.rem(lax.rem(zz, 2) + (dz + 1) // 2, 2)
        high = lax.rem(zz // 2 + dz // 2, 2)
        return high * 2 + low

    def index(zz, xx, cc):
        return zz * 8 + xx * 2 + cc

    def plane(zz, xx, cc):
        return (index(zz, xx, cc), cam, tp)

    right, left = lax.rem(x + 1, 4), lax.rem(x + 3, 4)
    sib = 1 - core
    z3, z1 = flip(z_lo, 2), flip(z_lo, 1)

    barrier = pltpu.get_barrier_semaphore()
    peers = [at_y(up), at_y(down), at_y(across), at_z(1), at_z(-1), at_z(3), at_z(-3), at_z(4)]
    for peer in peers:
        pl.semaphore_signal(barrier, inc=1, device_id=peer, device_id_type=MESH)

    @pl.loop(1, 32)
    def _(d):
        pl.semaphore_signal(
            barrier, inc=1, device_id=(lax.rem(seq + d, 32), cam, tp), device_id_type=MESH
        )

    loads = []
    for n, w in enumerate((wq_hbm, wk_hbm, wv_hbm)):
        loads.append(pltpu.make_async_copy(w, w_s.at[n], lsem.at[n]))
    loads.append(pltpu.make_async_copy(meta_ref, metag.at[0], lsem.at[3]))
    loads.append(pltpu.make_async_copy(gain_ref, gaing.at[0], lsem.at[4]))
    for half in range(2):
        loads.append(
            pltpu.make_async_copy(x_ref.at[half], xg.at[0, half, 0], lsem.at[5 + half])
        )
    for load in loads:
        load.start()
    acc[...] = jnp.zeros(acc.shape, F32)
    tot[...] = jnp.zeros(tot.shape, F32)
    top[...] = jnp.full(top.shape, START, F32)
    pl.semaphore_wait(barrier, len(peers) + 31)

    sent = []

    def describe(src, dst, send, recv, device):
        return pltpu.make_async_remote_copy(
            src_ref=src, dst_ref=dst, send_sem=send, recv_sem=recv, device_id=device,
            device_id_type=MESH,
        )

    def remote(src, dst, send, recv, device):
        copy = describe(src, dst, send, recv, device)
        copy.start()
        sent.append(copy)

    def received(ref, send, recv):
        describe(ref, ref, send, recv, at_y(up)).wait_recv()

    def piece(ref, c):
        return ref.at[pl.ds((c % 2) * ROWS, ROWS)]

    def z_out(f):
        for e in range(2):
            c = 2 * f + e
            target = ru if e == 0 else rd
            remote(
                piece(x_ref.at[f], c), target.at[f], zsend.at[c], zrecv.at[c],
                at_z(1) if e == 0 else at_z(-1),
            )

    def relay(f):
        for e in range(2):
            c = 2 * f + e
            ref = (ru if e == 0 else rd).at[f]
            received(ref, zsend.at[c], zrecv.at[c])
            remote(
                ref, piece(xg.at[1, f, 0], c), psend.at[c], precv.at[c],
                at_z(3) if e == 0 else at_z(-3),
            )

    def spread_y(source, p, c, toward):
        rel = 3 if toward == 0 else 1
        remote(
            source, piece(xg.at[p, c // 2, rel], c), xsend.at[p, toward, c],
            xrecv.at[p, rel, c], at_y(up if toward == 0 else down),
        )

    def own_y(f):
        for e in range(2):
            for toward in range(2):
                c = 2 * f + (1 - e if toward == 0 else e)
                spread_y(piece(x_ref.at[f], c), 0, c, toward)

    def got(p, rel, c):
        received(piece(xg.at[p, c // 2, rel], c), xsend.at[p, 0, c], xrecv.at[p, rel, c])

    def forward_y(p, f):
        for rel, c in ((3, 2 * f + 1), (1, 2 * f)):
            got(p, rel, c)
            ref = piece(xg.at[p, f, rel], c)
            remote(
                ref, piece(xg.at[p, f, 2], c), fsend.at[p, c], xrecv.at[p, 2, c],
                at_y(down if rel == 1 else up),
            )

    def rest_y(p, f):
        got(p, 3, 2 * f)
        got(p, 1, 2 * f + 1)
        got(p, 2, 2 * f)
        got(p, 2, 2 * f + 1)

    def partner(f):
        for e in range(2):
            c = 2 * f + e
            received(piece(xg.at[1, f, 0], c), psend.at[c], precv.at[c])
        for e in range(2):
            for toward in range(2):
                c = 2 * f + (1 - e if toward == 0 else e)
                spread_y(piece(xg.at[1, f, 0], c), 1, c, toward)

    def build_mixing(half):
        token = lax.broadcasted_iota(jnp.int32, (CELLS, 128), 0).astype(F32)
        for rel in range(4):
            block = metag[rel][:, half * 128 : half * 128 + 128]
            total = jnp.zeros((CELLS, 128), F32)
            for k in range(4):
                hit = token == block[4 + k : 5 + k, :]
                total = total + jnp.where(hit, block[k : k + 1, :], 0.0)
            first = total.astype(BF)
            mix[half, 0, :, rel * 128 : rel * 128 + 128] = first
            mix[half, 1, :, rel * 128 : rel * 128 + 128] = (
                total - first.astype(F32)
            ).astype(BF)

    def pool(p, f):
        rows = xg[p, f].reshape(4 * 128, HALF)
        bev[p, f] = jnp.dot(mix[f, 0], rows, preferred_element_type=F32) + jnp.dot(
            mix[f, 1], rows, preferred_element_type=F32
        )

    own = pl.multiple_of(tp * HALF, HALF)
    other = pl.multiple_of((1 - tp) * HALF, HALF)
    me = seq

    def project(f):
        step = 128
        for n in range(CELLS // step):
            a = bev[0, f, n * step : (n + 1) * step, :]
            b = bev[1, f, n * step : (n + 1) * step, :]
            squares = jnp.sum(a * a + b * b, axis=1, keepdims=True)
            scale = lax.rsqrt(squares / D + EPS)
            nrm[0, n * step : (n + 1) * step, :] = (a * scale * gaing[0]).astype(BF)
            nrm[1, n * step : (n + 1) * step, :] = (b * scale * gaing[1]).astype(BF)

    def multiply(f, n):
        result = jnp.dot(nrm[0], w_s[n, pl.ds(own, HALF), :], preferred_element_type=F32)
        result = result + jnp.dot(
            nrm[1], w_s[n, pl.ds(other, HALF), :], preferred_element_type=F32
        )
        for h in range(2):
            part = result[:, h * HD : (h + 1) * HD]
            mine = lax.rem(head + h, 2)
            if n == 0:
                qb[mine * 2, f] = part.astype(BF)
            elif n == 1:
                kvs[mine, f, 0] = part.astype(BF)
            else:
                flat = part.T.astype(BF)
                kvs[mine, f, 1, 0:HD, :] = flat[:, 0:HD]
                kvs[mine, f, 1, HD : 2 * HD, :] = flat[:, HD : 2 * HD]

    def own_copies(f):
        return [
            describe(kvs.at[1, f], kvb.at[me, f], bpre_s.at[f], bpre_r.at[f], plane(z3, x, core)),
            describe(
                kvs.at[0, f], kvb.at[me, f], bz_s.at[f, 0], bz_r.at[f, 0], plane(z1, x, core)
            ),
            describe(qb.at[2, f], qb.at[1, f], bq_s.at[f], bq_r.at[f], (31 - seq, cam, tp)),
        ]

    def issue_own(f):
        multiply(f, 1)
        multiply(f, 2)
        keep_copy = pltpu.make_async_copy(kvs.at[0, f], kvb.at[me, f], lc.at[f])
        keep_copy.start()
        copies = own_copies(f)
        copies[0].start()
        copies[1].start()
        keep_copy.wait()
        if f == 0:
            stage0(lax.rem(seq, 1))
        multiply(f, 0)
        copies[2].start()

    def unit(dz, dx, cc):
        return index(flip(z_lo, dz), lax.rem(x + dx, 4), cc)

    def x_copy(n, toward, kv):
        ref = kvb.at[unit(lax.rem(n, 4), 0, core), n // 4, kv]
        return describe(
            ref, ref, bx_s.at[n, toward, kv], bx_r.at[n, 3 if toward == 0 else 1, kv],
            plane(z_lo, right if toward == 0 else left, core),
        )

    def f_copy(n, kv):
        ref = kvb.at[unit(lax.rem(n, 4), 3 if kv == 1 else 1, core), n // 4, kv]
        return describe(
            ref, ref, bf_s.at[n, kv], bx_r.at[n, 2, kv],
            plane(z_lo, right if kv == 1 else left, core),
        )

    def c_copy(n, dx):
        ref = kvb.at[unit(lax.rem(n, 4), dx, core), n // 4]
        return describe(ref, ref, bc_s.at[n, dx], bc_r.at[n, dx], plane(z_lo, x, sib))

    def z_copy(f):
        ref = kvb.at[unit(2, 0, core), f]
        return describe(ref, ref, bz_s.at[f, 1], bz_r.at[f, 1], plane(z1, x, core))

    def arrived(n, rel, kv):
        ref = kvb.at[unit(lax.rem(n, 4), rel, core), n // 4, kv]
        received(ref, bx_s.at[n, 0, kv], bx_r.at[n, rel, kv])

    def stage0(n):
        f, dz = n // 4, lax.rem(n, 4)

        @pl.when(dz == 1)
        def _():
            received(kvb.at[unit(1, 0, core), f], bz_s.at[f, 0], bz_r.at[f, 0])

        @pl.when(dz == 2)
        def _():
            received(kvb.at[unit(2, 0, core), f], bpre_s.at[f], bpre_r.at[f])
            z_copy(f).start()

        @pl.when(dz == 3)
        def _():
            received(kvb.at[unit(3, 0, core), f], bz_s.at[f, 1], bz_r.at[f, 1])

        x_copy(n, 0, 1).start()
        x_copy(n, 1, 0).start()
        x_copy(n, 0, 0).start()
        x_copy(n, 1, 1).start()
        c_copy(n, 0).start()

    def stage1(n):
        arrived(n, 3, 1)
        f_copy(n, 1).start()
        arrived(n, 1, 0)
        f_copy(n, 0).start()
        arrived(n, 3, 0)
        c_copy(n, 3).start()
        arrived(n, 1, 1)
        c_copy(n, 1).start()

    def stage2(n):
        arrived(n, 2, 0)
        arrived(n, 2, 1)
        c_copy(n, 2).start()

    def blocks(*work):
        scores = [
            lax.dot_general(
                keys, qb[b, fq], (((1,), (1,)), ((), ())), preferred_element_type=F32
            )
            for b, fq, keys, _, _ in work
        ]
        done = []
        for s, (b, fq, _, values, biases) in zip(scores, work):
            before = top[b, fq]
            peak = before
            parts = [s[n * CELLS : (n + 1) * CELLS, :] for n in range(len(biases))]
            for part, bias in zip(parts, biases):
                peak = jnp.maximum(peak, jnp.max(part, axis=0, keepdims=True) + bias)
            factor = jnp.exp2((before - peak) * SCALE)
            total = tot[b, fq] * factor
            pieces = []
            for part, bias in zip(parts, biases):
                e = jnp.exp2((part - (peak - bias)) * SCALE)
                total = total + jnp.sum(e, axis=0, keepdims=True)
                pieces.append(e.astype(BF))
            mixed = jnp.dot(values, jnp.concatenate(pieces, axis=0), preferred_element_type=F32)
            done.append((peak, total, factor, mixed))
        for (peak, total, factor, mixed), (b, fq, _, _, _) in zip(done, work):
            top[b, fq] = peak
            tot[b, fq] = total
            acc[b, fq] = acc[b, fq] * factor + mixed

    def turned(u, f):
        return jnp.concatenate([kvb[u, f, 1, 0:HD, :], kvb[u, f, 1, HD : 2 * HD, :]], axis=1)

    rows_of = (seq, 31 - seq)

    def attend(n, dx):
        dz = lax.rem(n, 4)
        received(kvb.at[unit(dz, dx, sib), n // 4], bc_s.at[n, dx], bc_r.at[n, dx])
        u = unit(dz, dx, 0)
        kept = [jnp.where(keep_ref[2 * u + m] > 0, 0.0, FAR) for m in range(4)]
        low, high = head, 1 - head
        low_row = jnp.minimum(rows_of[0], rows_of[1])
        high_row = jnp.maximum(rows_of[0], rows_of[1])

        def bias(m, fq, row):
            ahead = 2 * u + m
            mine = 2 * row + fq
            open_key = jnp.where(ahead < mine, kept[m], FAR)
            return jnp.where(ahead == mine, 0.0, open_key)

        def even(b, row):
            keys = jnp.concatenate([kvb[u, 0, 0], kvb[u + 1, 0, 0]], axis=0)
            values = jnp.concatenate([turned(u, 0), turned(u + 1, 0)], axis=1)
            return (b, 0, keys, values, [bias(0, 0, row), bias(2, 0, row)])

        def odd(b, row):
            some = jnp.concatenate([kvb[u, 1, 0], kvb[u + 1, 1, 0]], axis=0)
            some_v = jnp.concatenate([turned(u, 1), turned(u + 1, 1)], axis=1)
            keys = jnp.concatenate([kvb[u, 0, 0], kvb[u + 1, 0, 0], some], axis=0)
            values = jnp.concatenate([turned(u, 0), turned(u + 1, 0), some_v], axis=1)
            return [
                (b, 1, keys, values, [bias(m, 1, row) for m in (0, 2, 1, 3)]),
                (b, 0, some, some_v, [bias(m, 0, row) for m in (1, 3)]),
            ]

        @pl.when((u <= low_row) & (n < 4))
        def _():
            blocks(even(low, low_row), even(high, high_row))

        @pl.when((u > low_row) & (u <= high_row) & (n < 4))
        def _():
            blocks(even(high, high_row))

        @pl.when((u <= low_row) & (n >= 4))
        def _():
            blocks(*odd(low, low_row), *odd(high, high_row))

        @pl.when((u > low_row) & (u <= high_row) & (n >= 4))
        def _():
            blocks(*odd(high, high_row))

    z_out(0)
    remote(meta_ref, metag.at[3], msend.at[0], mrecv.at[0], at_y(up))
    remote(meta_ref, metag.at[1], msend.at[1], mrecv.at[1], at_y(down))
    remote(meta_ref, metag.at[2], msend.at[2], mrecv.at[2], at_y(across))
    remote(gain_ref, gaing.at[1], gsend, grecv, at_z(4))
    own_y(0)
    relay(0)
    z_out(1)
    forward_y(0, 0)
    own_y(1)
    for n, rel in enumerate((3, 1, 2)):
        received(metag.at[rel], msend.at[n], mrecv.at[n])
    for load in loads:
        load.wait()
    relay(1)
    build_mixing(0)
    forward_y(0, 1)
    partner(0)
    build_mixing(1)
    rest_y(0, 0)
    pool(0, 0)
    forward_y(1, 0)
    rest_y(0, 1)
    pool(0, 1)
    received(gaing.at[1], gsend, grecv)
    partner(1)
    rest_y(1, 0)
    pool(1, 0)
    project(0)
    issue_own(0)
    forward_y(1, 1)

    @pl.loop(0, 10)
    def _(it):
        @pl.when((it >= 1) & (it < 9))
        def _():
            stage1(it - 1)

        @pl.when((it >= 2) & (it < 10))
        def _():
            stage2(it - 2)

        @pl.when(it < 7)
        def _():
            stage0(it + 1)

        @pl.when(it == A_AT)
        def _():
            rest_y(1, 1)
            pool(1, 1)
            project(1)
            issue_own(1)

        @pl.when((it == 1) | (it == 5))
        def _():
            received(qb.at[1, it // 5], bq_s.at[it // 5], bq_r.at[it // 5])

        @pl.loop(0, 4)
        def _(j):
            n = it - 1 - j // 3
            dx = lax.rem(3 * j, 4) - lax.rem(j // 2, 2) + 2 * (j // 3)

            @pl.when((n >= 0) & (n < 8))
            def _():
                attend(n, dx)

    def target(device, b):
        return (31 - device if b else device), device // 16

    def push(d, b):
        peer = lax.rem(seq + d, 32)
        row, h = target(seq, b)
        return describe(ob.at[b, peer], r_ref.at[row, h], d_s, d_r, (peer, cam, tp))

    for b in range(2):
        outs = []
        for f in range(2):
            outs.append((acc[b, f] / tot[b, f]).T.reshape(32, 8, HD))
        ob[b] = jnp.concatenate(outs, axis=1).astype(BF)

        @pl.loop(1, 32)
        def _(d):
            push(d, b).start()

        row, h = target(seq, b)
        pltpu.make_async_copy(ob.at[b, seq], r_ref.at[row, h], d_r).start()

    for copy in sent:
        copy.wait_send()

    @pl.loop(0, 8)
    def _(n):
        for kv in range(2):
            for toward in range(2):
                x_copy(n, toward, kv).wait_send()
            f_copy(n, kv).wait_send()
        for dx in range(4):
            c_copy(n, dx).wait_send()

    for f in range(2):
        z_copy(f).wait_send()
        for copy in own_copies(f):
            copy.wait_send()

    gone = ob.at[:, pl.ds(0, 31)]
    pltpu.make_async_copy(gone, gone, d_s).wait()
    pltpu.make_async_copy(r_ref, r_ref, d_r).wait()


A_AT = 2
VMEM = pl.BlockSpec(memory_space=pltpu.VMEM)
ANY = pl.BlockSpec(memory_space=pl.ANY)
SMEM = pl.BlockSpec(memory_space=pltpu.SMEM)
DMA = pltpu.SemaphoreType.DMA
LIMIT = 60 * 1024 * 1024


def call_fused(x, meta, gain, keep, wq, wk, wv):
    return pl.pallas_call(
        fused,
        out_shape=jax.ShapeDtypeStruct((32, 2, 16, HD), BF),
        in_specs=[ANY, VMEM, VMEM, SMEM, ANY, ANY, ANY],
        out_specs=VMEM,
        scratch_shapes=[
            pltpu.VMEM((2, 2, 4, 128, HALF), BF),
            pltpu.VMEM((4, 8, PIX), F32),
            pltpu.VMEM((2, 1, HALF), F32),
            pltpu.VMEM((2, ROWS, HALF), BF),
            pltpu.VMEM((2, ROWS, HALF), BF),
            pltpu.VMEM((3, D, 2 * HD), BF),
            pltpu.VMEM((2, 2, CELLS, HALF), F32),
            pltpu.VMEM((2, CELLS, HALF), BF),
            pltpu.VMEM((2, 2, CELLS, 512), BF),
            pltpu.VMEM((32, 2, 2, CELLS, HD), BF),
            pltpu.VMEM((2, 2, 2, CELLS, HD), BF),
            pltpu.VMEM((3, 2, CELLS, HD), BF),
            pltpu.VMEM((2, 2, HD, CELLS), F32),
            pltpu.VMEM((2, 2, 1, CELLS), F32),
            pltpu.VMEM((2, 2, 1, CELLS), F32),
            pltpu.VMEM((2, 32, 16, HD), BF),
            DMA((2, 2, 4)), DMA((2, 4, 4)), DMA((4,)), DMA((4,)), DMA((4,)), DMA((4,)),
            DMA((2, 4)), DMA((3,)), DMA((3,)), DMA, DMA, DMA((7,)),
            DMA((2,)), DMA((2,)), DMA((2,)), DMA((2,)), DMA((2, 2)), DMA((2, 2)),
            DMA((8, 2, 2)), DMA((8, 4, 2)), DMA((8, 2)), DMA((8, 4)), DMA((8, 4)), DMA((2,)),
            DMA, DMA,
        ],
        compiler_params=pltpu.CompilerParams(
            collective_id=0, has_side_effects=True, vmem_limit_bytes=LIMIT
        ),
        name="fused",
    )(x, meta, gain, keep, wq, wk, wv)


def local(
    pixel_feature, depth_score, depth_bin, cell_owner, cell_local, frame_keep, norm_gain,
    w_query, w_key, w_value,
):
    prob = depth_score / jnp.sum(depth_score, axis=1, keepdims=True)
    bins = jnp.arange(depth_score.shape[1], dtype=jnp.int32)
    picked = jnp.sum(
        jnp.where(depth_bin[:, :, None] == bins[None, None, :], prob[:, None, :], 0.0), axis=2
    )
    weight = lax.reduce_precision(picked, 8, 7)
    cell = (cell_owner.reshape(PIX, 4) * 8 + cell_local).astype(F32)
    meta = jnp.concatenate([weight, cell], axis=1).T
    r = call_fused(
        pixel_feature.reshape(2, 128, HALF), meta, norm_gain.reshape(1, HALF), frame_keep,
        w_query, w_key, w_value,
    )
    r = r.reshape(32, 2, 2, 8, HD)
    out = r.transpose(3, 0, 2, 1, 4)
    return out.reshape(TOK, 2 * HD)


def solution(mesh):
    return jax.shard_map(
        local,
        mesh=mesh,
        in_specs=(
            P(("seq", "cam"), "tp"),
            P(("seq", "cam"), None),
            P(("seq", "cam"), None),
            P(("seq", "cam"), None),
            P(("seq", "cam"), None),
            P(),
            P("tp"),
            P(None, ("cam", "tp")),
            P(None, ("cam", "tp")),
            P(None, ("cam", "tp")),
        ),
        out_specs=P("seq", ("cam", "tp")),
        check_vma=False,
    )
```
